256 devices in a mesh: lon: 32 (over y, x, core), lat: 8 (over z).
Axes of the slice: x: 4, y: 4, z: 8, core: 2. Of those that a mesh axis runs over, the one named last changes fastest.
Arguments:
- tracer: float32 [4096, 8192], P('lon', 'lat'), parts along dimension 1, may hold values from -7 to 7
- lower2: float32 [4096, 8192], P('lon', 'lat'), parts along dimension 1, may hold values from -4096 to -256
- lower1: float32 [4096, 8192], P('lon', 'lat'), parts along dimension 1, may hold values from -6144 to -256
- upper1: float32 [4096, 8192], P('lon', 'lat'), parts along dimension 1, may hold values from -4096 to -128
- upper2: float32 [4096, 8192], P('lon', 'lat'), parts along dimension 1, may hold values from -2048 to -64
Outputs:
- advanced: float32 [4096, 8192], P('lon', 'lat'), parts along dimension 1
The draws below stay inside these ranges and needn't reach their ends.
There are 8 independent parts, one for each index of `lat`. The reference program is written for one: setup_inputs(seed, part) draws one part's arguments, and reference() takes and returns one part's arrays. A program takes and returns all parts, laid end to end along the dimension named above; each array names one. Nothing has to cross between parts.
All inputs are finite; a program needn't handle non-finite values.
Results may differ from the reference program's by a relative error of at most 0.0003.
Values sent between devices are 32-bit elements; how exact they have to be, the bound alone decides.
No kernel may reach another device: no remote copies, remote signals or barrier semaphores. Data moves between devices by JAX's collectives and lax.ppermute only.
A program may use at most 128 MiB of HBM per device.

```python
import math
import jax
import jax.numpy as jnp
from jax import lax

NLON = 4096
LINES = 1024
HSCALE = 2048


def coupling(key, salt, weight):
    inner_key = jax.random.fold_in(key, salt)
    key_wave, key_phase, key_rough = jax.random.split(inner_key, 3)
    position = jnp.arange(NLON, dtype=jnp.float32)[:, None] / NLON
    wave_number = jax.random.randint(key_wave, (1, LINES), 1, 4).astype(jnp.float32)
    phase_shift = jax.random.uniform(key_phase, (1, LINES), jnp.float32, 0.0, 2.0 * math.pi)
    envelope = jnp.exp(0.6 * jnp.sin(2.0 * math.pi * wave_number * position + phase_shift))
    rough_part = jax.random.uniform(key_rough, (NLON, LINES), jnp.float32, 0.6, 1.8)
    return (-(weight * HSCALE) * envelope * rough_part).astype(jnp.float32)


def draw_lower2(key, part):
    return coupling(key, 11, 0.5)


def draw_lower1(key, part):
    return coupling(key, 12, 0.7)


def draw_upper1(key, part):
    return coupling(key, 13, 0.4)


def draw_upper2(key, part):
    return coupling(key, 14, 0.2)


def draw_tracer(key, part):
    inner_key = jax.random.fold_in(key, 21)
    key_rough, key_first, key_second, phase_first, phase_second = jax.random.split(inner_key, 5)
    position = jnp.arange(NLON, dtype=jnp.float32)[:, None] / NLON
    wave_first = jax.random.randint(key_first, (1, LINES), 1, 9).astype(jnp.float32)
    wave_second = jax.random.randint(key_second, (1, LINES), 1, 9).astype(jnp.float32)
    shift_first = jax.random.uniform(phase_first, (1, LINES), jnp.float32, 0.0, 2.0 * math.pi)
    shift_second = jax.random.uniform(phase_second, (1, LINES), jnp.float32, 0.0, 2.0 * math.pi)
    smooth_part = 0.8 * jnp.sin(2.0 * math.pi * wave_first * position + shift_first) + 0.8 * jnp.sin(2.0 * math.pi * wave_second * position + shift_second)
    rough_part = jnp.clip(jax.random.normal(key_rough, (NLON, LINES), jnp.float32), -5.0, 5.0)
    return (smooth_part + rough_part).astype(jnp.float32)


def setup_inputs(seed: int = 0, part: int = 0) -> dict:
    streams_of = jax.random.split(jax.random.key(seed), 6)
    own_keys = jax.random.split(jax.random.fold_in(streams_of[5], part), 6)
    return {
        "tracer": draw_tracer(jax.random.fold_in(jax.random.fold_in(streams_of[5], part), 71), part),
        "lower2": draw_lower2(jax.random.fold_in(jax.random.fold_in(streams_of[5], part), 71), part),
        "lower1": draw_lower1(jax.random.fold_in(jax.random.fold_in(streams_of[5], part), 71), part),
        "upper1": draw_upper1(jax.random.fold_in(jax.random.fold_in(streams_of[5], part), 71), part),
        "upper2": draw_upper2(jax.random.fold_in(jax.random.fold_in(streams_of[5], part), 71), part),
    }


def reference(tracer, lower2, lower1, upper1, upper2):
    diagonal = 1.0 + (jnp.abs(lower2) + jnp.abs(lower1) + jnp.abs(upper1) + jnp.abs(upper2))
    padded = jnp.pad(tracer, ((2, 2), (0, 0)))
    applied = lower2 * padded[0:-4] + lower1 * padded[1:-3] + diagonal * tracer + upper1 * padded[3:-1] + upper2 * padded[4:]
    source = 2.0 * tracer - applied
    zero_row = jnp.zeros_like(tracer[0])

    def forward(state, row_data):
        last_p, last_q, last_g, older_p, older_q, older_g = state
        far_low, near_low, centre, near_high, far_high, target = row_data
        beta_term = near_low - far_low * older_p
        pivot_value = centre - far_low * older_q - beta_term * last_p
        new_p = (near_high - beta_term * last_q) / pivot_value
        new_q = far_high / pivot_value
        new_g = (target - far_low * older_g - beta_term * last_g) / pivot_value
        return (new_p, new_q, new_g, last_p, last_q, last_g), (new_p, new_q, new_g)

    start_state = (zero_row, zero_row, zero_row, zero_row, zero_row, zero_row)
    _, (coef_p, coef_q, coef_g) = lax.scan(forward, start_state, (lower2, lower1, diagonal, upper1, upper2, source))

    def backward(state, row_data):
        after_one, after_two = state
        factor_p, factor_q, factor_g = row_data
        solved = factor_g - factor_p * after_one - factor_q * after_two
        return (solved, after_one), solved

    _, advanced = lax.scan(backward, (zero_row, zero_row), (coef_p, coef_q, coef_g), reverse=True)
    return advanced
```

```python
import jax
import jax.numpy as jnp
from jax import lax
from jax.experimental import pallas as pl
from jax.experimental.pallas import tpu as pltpu
from jax.sharding import PartitionSpec as P

ROWS = 128
SUBS = 4
CHUNKS = 4
TILE = (8, 128)
VMEM_BYTES = 12 << 20


def eliminate(state, coefs):
    (far_g, far_a, far_b, far_p, far_q), (near_g, near_a, near_b, near_p, near_q) = state
    low2, low1, up1, up2, target = coefs
    minus_diag = (((low2 + low1) + up1) + up2) - 1.0
    beta = low1 + low2 * far_p
    scale = pl.reciprocal(minus_diag - low2 * far_q - beta * near_p)
    new_g = (low2 * far_g + beta * near_g - target) * scale
    new_a = (low2 * far_a + beta * near_a) * scale
    new_b = (low2 * far_b + beta * near_b) * scale
    new_p = (up1 + beta * near_q) * scale
    new_q = up2 * scale
    return (new_g, new_a, new_b, new_p, new_q)


def eliminate_first(coefs):
    low2, low1, up1, up2, target = coefs
    scale = pl.reciprocal((((low2 + low1) + up1) + up2) - 1.0)
    return (-target * scale, low2 * scale, low1 * scale, up1 * scale, up2 * scale)


def eliminate_second(first, coefs):
    near_g, near_a, near_b, near_p, near_q = first
    low2, low1, up1, up2, target = coefs
    scale = pl.reciprocal((((low2 + low1) + up1) + up2) - 1.0 - low1 * near_p)
    return (
        (low1 * near_g - target) * scale,
        low1 * near_a * scale,
        (low2 + low1 * near_b) * scale,
        (up1 + low1 * near_q) * scale,
        up2 * scale,
    )


def carry_on(head, row):
    g, a, b, p, q = head
    row_g, row_a, row_b, row_p, row_q = row
    return (g + p * row_g, a + p * row_a, b + p * row_b, q + p * row_p, p * row_q)


def affine(row, w, e):
    return row[0] + row[1] * w[0] + row[2] * w[1] + row[3] * e[0] + row[4] * e[1]


def mix(row, left, right):
    return tuple(row[0] * x + row[1] * y for x, y in zip(left, right))


def split_of(first, second):
    r0, r1 = first[2], first[3]
    l0, l1 = second[0], second[1]
    n00 = r0[3] * l0[1] + r0[4] * l1[1]
    n01 = r0[3] * l0[2] + r0[4] * l1[2]
    n10 = r1[3] * l0[1] + r1[4] * l1[1]
    n11 = r1[3] * l0[2] + r1[4] * l1[2]
    d00 = 1.0 - n00
    d11 = 1.0 - n11
    inv = pl.reciprocal(d00 * d11 - n01 * n10)
    k0 = (d11 * inv, n01 * inv)
    k1 = (n10 * inv, d00 * inv)
    s0 = (r0[0] + r0[3] * l0[0] + r0[4] * l1[0], r0[1], r0[2]) + mix(r0[3:5], l0[3:5], l1[3:5])
    s1 = (r1[0] + r1[3] * l0[0] + r1[4] * l1[0], r1[1], r1[2]) + mix(r1[3:5], l0[3:5], l1[3:5])
    a0 = mix(k0, s0, s1)
    a1 = mix(k1, s0, s1)
    b0 = mix(l0[1:3], a0, a1)
    b1 = mix(l1[1:3], a0, a1)
    b0 = (b0[0] + l0[0], b0[1], b0[2], b0[3] + l0[3], b0[4] + l0[4])
    b1 = (b1[0] + l1[0], b1[1], b1[2], b1[3] + l1[3], b1[4] + l1[4])
    return (a0, a1, b0, b1)


def join(first, second, split):
    a0, a1, b0, b1 = split
    left, right = [], []
    for row in first[0:2]:
        far = mix(row[3:5], b0, b1)
        left.append((row[0] + far[0], row[1] + far[1], row[2] + far[2], far[3], far[4]))
    for row in second[2:4]:
        far = mix(row[1:3], a0, a1)
        right.append((row[0] + far[0], far[1], far[2], row[3] + far[3], row[4] + far[4]))
    return tuple(left + right)


def read_port(ref):
    return tuple(tuple(ref[5 * i + j] for j in range(5)) for i in range(4))


def write_port(ref, port):
    for i in range(4):
        for j in range(5):
            ref[5 * i + j] = port[i][j]


def swap_if(flag, one, two):
    first = tuple(tuple(jnp.where(flag, y, x) for x, y in zip(u, v)) for u, v in zip(one, two))
    second = tuple(tuple(jnp.where(flag, x, y) for x, y in zip(u, v)) for u, v in zip(one, two))
    return first, second


def row_of(buffers, sub, chunk, step):
    return tuple(buf[sub, chunk, pl.ds(step, 8, stride=8), :] for buf in buffers)


def port_kernel(*refs):
    sources, out, buffers, sems = refs[0:5], refs[5], refs[6:11], refs[11]
    copies = [
        [
            pltpu.make_async_copy(src.at[:, c], buf.at[:, c], sems.at[i, c])
            for i, (src, buf) in enumerate(zip(sources, buffers))
        ]
        for c in range(CHUNKS)
    ]
    for group in copies:
        for copy in group:
            copy.start()
    far, near = [None] * SUBS, [None] * SUBS
    head0, head1 = [None] * SUBS, [None] * SUBS
    for c in range(CHUNKS):
        for copy in copies[c]:
            copy.wait()
        for step in range(8):
            for s in range(SUBS):
                coefs = row_of(buffers, s, c, step)
                if c == 0 and step == 0:
                    near[s] = eliminate_first(coefs)
                    head0[s] = near[s]
                    continue
                if c == 0 and step == 1:
                    row = eliminate_second(near[s], coefs)
                    head1[s] = row
                else:
                    row = eliminate((far[s], near[s]), coefs)
                    head1[s] = carry_on(head1[s], row)
                head0[s] = carry_on(head0[s], row)
                far[s], near[s] = near[s], row
    ports = []
    for s in range(SUBS):
        g, a, b, p, q = far[s]
        row = near[s]
        tail0 = (g + p * row[0], a + p * row[1], b + p * row[2], q + p * row[3], p * row[4])
        ports.append((head0[s], head1[s], tail0, row))
    while len(ports) > 1:
        ports = [
            join(ports[i], ports[i + 1], split_of(ports[i], ports[i + 1]))
            for i in range(0, len(ports), 2)
        ]
    write_port(out, ports[0])


def spikes_kernel(l2, l1, u1, u2, tr, after, out, p_buf, q_buf):
    buffers = (l2, l1, u1, u2, tr)
    far, near = None, None
    for i in range(ROWS):
        coefs = row_of(buffers, i // 32, (i // 8) % 4, i % 8)
        if i == 0:
            row = eliminate_first(coefs)
        elif i == 1:
            row = eliminate_second(near, coefs)
        else:
            row = eliminate((far, near), coefs)
        out[0, i], out[1, i], out[2, i] = row[0], row[1], row[2]
        p_buf[i], q_buf[i] = row[3], row[4]
        far, near = near, row
    zero = jnp.zeros(TILE, jnp.float32)
    one = jnp.ones(TILE, jnp.float32)
    next1 = (zero, zero, zero, one, zero)
    next2 = (zero, zero, zero, zero, one)
    for i in reversed(range(ROWS)):
        p, q = p_buf[i], q_buf[i]
        own = mix((p, q), next1, next2)
        own = (own[0] + out[0, i], own[1] + out[1, i], own[2] + out[2, i], own[3], own[4])
        target = tr[i // 32, (i // 8) % 4, pl.ds(i % 8, 8, stride=8), :]
        out[0, i] = own[0] + own[0] - target
        for k in range(1, 5):
            out[k, i] = own[k]
        next2 = next1
        next1 = own


def core_kernel(own_ref, other_ref, out, split_out):
    is_high = lax.axis_index("lon") % 2 == 1
    first, second = swap_if(is_high, read_port(own_ref), read_port(other_ref))
    split = split_of(first, second)
    write_port(split_out, split)
    write_port(out, join(first, second, split))


def bits(divisor):
    place = (lax.axis_index("lon") // divisor) % 4
    return place % 2 == 1, place // 2 == 1


def group_kernel(own_ref, by1, by2, by3, out, split_pair, split_top):
    low_bit, high_bit = bits(2)
    first, second = swap_if(low_bit, read_port(own_ref), read_port(by1))
    split = split_of(first, second)
    write_port(split_pair, split)
    mine = join(first, second, split)
    first, second = swap_if(low_bit, read_port(by2), read_port(by3))
    theirs = join(first, second, split_of(first, second))
    first, second = swap_if(high_bit, mine, theirs)
    split = split_of(first, second)
    write_port(split_top, split)
    write_port(out, join(first, second, split))


def descend(flag, split, w, e):
    a0, a1 = affine(split[0], w, e), affine(split[1], w, e)
    b0, b1 = affine(split[2], w, e), affine(split[3], w, e)
    new_w = (jnp.where(flag, a0, w[0]), jnp.where(flag, a1, w[1]))
    new_e = (jnp.where(flag, e[0], b0), jnp.where(flag, e[1], b1))
    return new_w, new_e


def final_kernel(own_ref, by1, by2, by3, top_x, pair_x, core, spikes, out, stage, sems):
    low_bit, high_bit = bits(8)
    first, second = swap_if(low_bit, read_port(own_ref), read_port(by1))
    split_mine = split_of(first, second)
    mine = join(first, second, split_mine)
    first, second = swap_if(low_bit, read_port(by2), read_port(by3))
    theirs = join(first, second, split_of(first, second))
    first, second = swap_if(high_bit, mine, theirs)
    zero = jnp.zeros(TILE, jnp.float32)
    w, e = (zero, zero), (zero, zero)
    w, e = descend(high_bit, split_of(first, second), w, e)
    w, e = descend(low_bit, split_mine, w, e)
    low_bit, high_bit = bits(2)
    w, e = descend(high_bit, read_port(top_x), w, e)
    w, e = descend(low_bit, read_port(pair_x), w, e)
    w, e = descend(lax.axis_index("lon") % 2 == 1, read_port(core), w, e)
    weights = (w[0] + w[0], w[1] + w[1], e[0] + e[0], e[1] + e[1])
    copies = []
    for s in range(SUBS):
        for c in range(CHUNKS):
            for step in range(8):
                i = 32 * s + 8 * c + step
                value = spikes[0, i]
                for k in range(4):
                    value = value + spikes[k + 1, i] * weights[k]
                stage[s, c, pl.ds(step, 8, stride=8), :] = value
        copy = pltpu.make_async_copy(stage.at[s], out.at[s], sems.at[s])
        copy.start()
        copies.append(copy)
    for copy in copies:
        copy.wait()


def call(kernel, outs, operands, out_specs=None, in_specs=None, scratch=(), name=None):
    vmem = pl.BlockSpec(memory_space=pltpu.VMEM)
    return pl.pallas_call(
        kernel,
        out_shape=[jax.ShapeDtypeStruct(shape, jnp.float32) for shape in outs],
        in_specs=in_specs or [vmem] * len(operands),
        out_specs=out_specs or [vmem] * len(outs),
        scratch_shapes=list(scratch),
        compiler_params=pltpu.CompilerParams(vmem_limit_bytes=VMEM_BYTES),
        name=name,
    )(*operands)


def exchange(port, bit_mask):
    return lax.ppermute(port, "lon", [(i, i ^ bit_mask) for i in range(32)])


def per_device(tracer, lower2, lower1, upper1, upper2):
    vmem = pl.BlockSpec(memory_space=pltpu.VMEM)
    hbm = pl.BlockSpec(memory_space=pltpu.HBM)
    tiles = (SUBS, CHUNKS, 64, 128)

    def view(array):
        return array.reshape(16, 8, 8, 128).transpose(0, 2, 1, 3).reshape(tiles)

    arrays = [
        pltpu.with_memory_space_constraint(view(a), pltpu.HBM)
        for a in (lower2, lower1, upper1, upper2, tracer)
    ]
    port_shape = (20,) + TILE
    port, *loaded = call(
        port_kernel,
        [port_shape] + [tiles] * 5,
        arrays,
        in_specs=[hbm] * 5,
        scratch=[pltpu.SemaphoreType.DMA((5, CHUNKS))],
        name="segment_port",
    )
    chip, core_split = call(core_kernel, [port_shape] * 2, [port, exchange(port, 1)], name="core_join")
    by_x = [exchange(chip, k) for k in (2, 4, 6)]
    (spikes,) = call(
        spikes_kernel,
        [(5, ROWS) + TILE],
        loaded + [chip],
        scratch=[pltpu.VMEM((ROWS,) + TILE, jnp.float32)] * 2,
        name="segment_spikes",
    )
    group, pair_x, top_x = call(group_kernel, [port_shape] * 3, [chip] + by_x, name="x_join")
    by_y = [exchange(group, k) for k in (8, 16, 24)]
    (out,) = call(
        final_kernel,
        [tiles],
        [group] + by_y + [top_x, pair_x, core_split, spikes],
        out_specs=[hbm],
        scratch=[pltpu.VMEM(tiles, jnp.float32), pltpu.SemaphoreType.DMA((SUBS,))],
        name="combine",
    )
    return out.reshape(16, 8, 8, 128).transpose(0, 2, 1, 3).reshape(ROWS, 1024)


def solution(mesh):
    spec = P("lon", "lat")
    return jax.shard_map(
        per_device, mesh=mesh, in_specs=(spec,) * 5, out_specs=spec, check_vma=False
    )
```

```python
import jax
import jax.numpy as jnp
from jax import lax
from jax.experimental import pallas as pl
from jax.experimental.pallas import tpu as pltpu
from jax.sharding import PartitionSpec as P

ROWS = 128
SUBS = 4
CHUNKS = 4
TILE = (8, 128)
VMEM_BYTES = 12 << 20


def eliminate(state, coefs):
    (far_g, far_a, far_b, far_p, far_q), (near_g, near_a, near_b, near_p, near_q) = state
    low2, low1, up1, up2, target = coefs
    minus_diag = (((low2 + low1) + up1) + up2) - 1.0
    beta = low1 + low2 * far_p
    scale = pl.reciprocal(minus_diag - low2 * far_q - beta * near_p)
    new_g = (low2 * far_g + beta * near_g - target) * scale
    new_a = (low2 * far_a + beta * near_a) * scale
    new_b = (low2 * far_b + beta * near_b) * scale
    new_p = (up1 + beta * near_q) * scale
    new_q = up2 * scale
    return (new_g, new_a, new_b, new_p, new_q)


def eliminate_first(coefs):
    low2, low1, up1, up2, target = coefs
    scale = pl.reciprocal((((low2 + low1) + up1) + up2) - 1.0)
    return (-target * scale, low2 * scale, low1 * scale, up1 * scale, up2 * scale)


def eliminate_second(first, coefs):
    near_g, near_a, near_b, near_p, near_q = first
    low2, low1, up1, up2, target = coefs
    scale = pl.reciprocal((((low2 + low1) + up1) + up2) - 1.0 - low1 * near_p)
    return (
        (low1 * near_g - target) * scale,
        low1 * near_a * scale,
        (low2 + low1 * near_b) * scale,
        (up1 + low1 * near_q) * scale,
        up2 * scale,
    )


def carry_on(head, row):
    g, a, b, p, q = head
    row_g, row_a, row_b, row_p, row_q = row
    return (g + p * row_g, a + p * row_a, b + p * row_b, q + p * row_p, p * row_q)


def affine(row, w, e):
    return row[0] + row[1] * w[0] + row[2] * w[1] + row[3] * e[0] + row[4] * e[1]


def mix(row, left, right):
    return tuple(row[0] * x + row[1] * y for x, y in zip(left, right))


def split_of(first, second):
    r0, r1 = first[2], first[3]
    l0, l1 = second[0], second[1]
    n00 = r0[3] * l0[1] + r0[4] * l1[1]
    n01 = r0[3] * l0[2] + r0[4] * l1[2]
    n10 = r1[3] * l0[1] + r1[4] * l1[1]
    n11 = r1[3] * l0[2] + r1[4] * l1[2]
    d00 = 1.0 - n00
    d11 = 1.0 - n11
    inv = pl.reciprocal(d00 * d11 - n01 * n10)
    k0 = (d11 * inv, n01 * inv)
    k1 = (n10 * inv, d00 * inv)
    s0 = (r0[0] + r0[3] * l0[0] + r0[4] * l1[0], r0[1], r0[2]) + mix(r0[3:5], l0[3:5], l1[3:5])
    s1 = (r1[0] + r1[3] * l0[0] + r1[4] * l1[0], r1[1], r1[2]) + mix(r1[3:5], l0[3:5], l1[3:5])
    a0 = mix(k0, s0, s1)
    a1 = mix(k1, s0, s1)
    b0 = mix(l0[1:3], a0, a1)
    b1 = mix(l1[1:3], a0, a1)
    b0 = (b0[0] + l0[0], b0[1], b0[2], b0[3] + l0[3], b0[4] + l0[4])
    b1 = (b1[0] + l1[0], b1[1], b1[2], b1[3] + l1[3], b1[4] + l1[4])
    return (a0, a1, b0, b1)


def join(first, second, split):
    a0, a1, b0, b1 = split
    left, right = [], []
    for row in first[0:2]:
        far = mix(row[3:5], b0, b1)
        left.append((row[0] + far[0], row[1] + far[1], row[2] + far[2], far[3], far[4]))
    for row in second[2:4]:
        far = mix(row[1:3], a0, a1)
        right.append((row[0] + far[0], far[1], far[2], row[3] + far[3], row[4] + far[4]))
    return tuple(left + right)


def read_port(ref):
    return tuple(tuple(ref[5 * i + j] for j in range(5)) for i in range(4))


def write_port(ref, port):
    for i in range(4):
        for j in range(5):
            ref[5 * i + j] = port[i][j]


def swap_if(flag, one, two):
    first = tuple(tuple(jnp.where(flag, y, x) for x, y in zip(u, v)) for u, v in zip(one, two))
    second = tuple(tuple(jnp.where(flag, x, y) for x, y in zip(u, v)) for u, v in zip(one, two))
    return first, second


def row_of(buffers, sub, chunk, step):
    return tuple(buf[sub, chunk, pl.ds(step, 8, stride=8), :] for buf in buffers)


def port_kernel(*refs):
    sources, out, buffers, sems = refs[0:5], refs[5], refs[6:11], refs[11]
    copies = [
        [
            pltpu.make_async_copy(src.at[:, c], buf.at[:, c], sems.at[i, c])
            for i, (src, buf) in enumerate(zip(sources, buffers))
        ]
        for c in range(CHUNKS)
    ]
    for group in copies:
        for copy in group:
            copy.start()
    far, near = [None] * SUBS, [None] * SUBS
    head0, head1 = [None] * SUBS, [None] * SUBS
    for c in range(CHUNKS):
        for copy in copies[c]:
            copy.wait()
        for step in range(8):
            for s in range(SUBS):
                coefs = row_of(buffers, s, c, step)
                if c == 0 and step == 0:
                    near[s] = eliminate_first(coefs)
                    head0[s] = near[s]
                    continue
                if c == 0 and step == 1:
                    row = eliminate_second(near[s], coefs)
                    head1[s] = row
                else:
                    row = eliminate((far[s], near[s]), coefs)
                    head1[s] = carry_on(head1[s], row)
                head0[s] = carry_on(head0[s], row)
                far[s], near[s] = near[s], row
    ports = []
    for s in range(SUBS):
        g, a, b, p, q = far[s]
        row = near[s]
        tail0 = (g + p * row[0], a + p * row[1], b + p * row[2], q + p * row[3], p * row[4])
        ports.append((head0[s], head1[s], tail0, row))
    while len(ports) > 1:
        ports = [
            join(ports[i], ports[i + 1], split_of(ports[i], ports[i + 1]))
            for i in range(0, len(ports), 2)
        ]
    write_port(out, ports[0])


def spikes_kernel(l2, l1, u1, u2, tr, after, out, p_buf, q_buf):
    buffers = (l2, l1, u1, u2, tr)
    far, near = None, None
    for i in range(ROWS):
        coefs = row_of(buffers, i // 32, (i // 8) % 4, i % 8)
        if i == 0:
            row = eliminate_first(coefs)
        elif i == 1:
            row = eliminate_second(near, coefs)
        else:
            row = eliminate((far, near), coefs)
        out[0, i], out[1, i], out[2, i] = row[0], row[1], row[2]
        p_buf[i], q_buf[i] = row[3], row[4]
        far, near = near, row
    zero = jnp.zeros(TILE, jnp.float32)
    one = jnp.ones(TILE, jnp.float32)
    next1 = (zero, zero, zero, one, zero)
    next2 = (zero, zero, zero, zero, one)
    for i in reversed(range(ROWS)):
        p, q = p_buf[i], q_buf[i]
        own = mix((p, q), next1, next2)
        own = (own[0] + out[0, i], own[1] + out[1, i], own[2] + out[2, i], own[3], own[4])
        target = tr[i // 32, (i // 8) % 4, pl.ds(i % 8, 8, stride=8), :]
        out[0, i] = own[0] + own[0] - target
        for k in range(1, 5):
            out[k, i] = own[k]
        next2 = next1
        next1 = own


def core_kernel(own_ref, other_ref, out, split_out):
    is_high = lax.axis_index("lon") % 2 == 1
    first, second = swap_if(is_high, read_port(own_ref), read_port(other_ref))
    split = split_of(first, second)
    write_port(split_out, split)
    write_port(out, join(first, second, split))


def bits(divisor):
    place = (lax.axis_index("lon") // divisor) % 4
    return place % 2 == 1, place // 2 == 1


def group_kernel(own_ref, by1, by2, by3, out, split_pair, split_top):
    low_bit, high_bit = bits(2)
    first, second = swap_if(low_bit, read_port(own_ref), read_port(by1))
    split = split_of(first, second)
    write_port(split_pair, split)
    mine = join(first, second, split)
    first, second = swap_if(low_bit, read_port(by2), read_port(by3))
    theirs = join(first, second, split_of(first, second))
    first, second = swap_if(high_bit, mine, theirs)
    split = split_of(first, second)
    write_port(split_top, split)
    write_port(out, join(first, second, split))


def descend(flag, split, w, e):
    a0, a1 = affine(split[0], w, e), affine(split[1], w, e)
    b0, b1 = affine(split[2], w, e), affine(split[3], w, e)
    new_w = (jnp.where(flag, a0, w[0]), jnp.where(flag, a1, w[1]))
    new_e = (jnp.where(flag, e[0], b0), jnp.where(flag, e[1], b1))
    return new_w, new_e


def solve_kernel(own_ref, by1, by2, by3, top_x, pair_x, core, before, low_out, high_out):
    low_bit, high_bit = bits(8)
    first, second = swap_if(low_bit, read_port(own_ref), read_port(by1))
    split_mine = split_of(first, second)
    mine = join(first, second, split_mine)
    first, second = swap_if(low_bit, read_port(by2), read_port(by3))
    theirs = join(first, second, split_of(first, second))
    first, second = swap_if(high_bit, mine, theirs)
    zero = jnp.zeros(TILE, jnp.float32)
    w, e = (zero, zero), (zero, zero)
    w, e = descend(high_bit, split_of(first, second), w, e)
    w, e = descend(low_bit, split_mine, w, e)
    low_bit, high_bit = bits(2)
    w, e = descend(high_bit, read_port(top_x), w, e)
    w, e = descend(low_bit, read_port(pair_x), w, e)
    a0, a1, b0, b1 = (affine(row, w, e) for row in read_port(core))
    for k, value in enumerate((w[0], w[1], b0, b1)):
        low_out[k] = value + value
    for k, value in enumerate((a0, a1, e[0], e[1])):
        high_out[k] = value + value


def combine_kernel(received, high_own, spikes, out, stage, sems):
    is_high = lax.axis_index("lon") % 2 == 1
    weights = [jnp.where(is_high, high_own[k], received[k]) for k in range(4)]
    copies = []
    for s in range(SUBS):
        for c in range(CHUNKS):
            for step in range(8):
                i = 32 * s + 8 * c + step
                value = spikes[0, i]
                for k in range(4):
                    value = value + spikes[k + 1, i] * weights[k]
                stage[s, c, pl.ds(step, 8, stride=8), :] = value
        copy = pltpu.make_async_copy(stage.at[s], out.at[s], sems.at[s])
        copy.start()
        copies.append(copy)
    for copy in copies:
        copy.wait()


def call(kernel, outs, operands, out_specs=None, in_specs=None, scratch=(), name=None):
    vmem = pl.BlockSpec(memory_space=pltpu.VMEM)
    return pl.pallas_call(
        kernel,
        out_shape=[jax.ShapeDtypeStruct(shape, jnp.float32) for shape in outs],
        in_specs=in_specs or [vmem] * len(operands),
        out_specs=out_specs or [vmem] * len(outs),
        scratch_shapes=list(scratch),
        compiler_params=pltpu.CompilerParams(vmem_limit_bytes=VMEM_BYTES),
        name=name,
    )(*operands)


def exchange(port, odd_mask, even_mask):
    pairs = [(i, i ^ (odd_mask if i % 2 else even_mask)) for i in range(32)]
    return lax.ppermute(port, "lon", pairs)


def per_device(tracer, lower2, lower1, upper1, upper2):
    vmem = pl.BlockSpec(memory_space=pltpu.VMEM)
    hbm = pl.BlockSpec(memory_space=pltpu.HBM)
    tiles = (SUBS, CHUNKS, 64, 128)

    def view(array):
        return array.reshape(16, 8, 8, 128).transpose(0, 2, 1, 3).reshape(tiles)

    arrays = [
        pltpu.with_memory_space_constraint(view(a), pltpu.HBM)
        for a in (lower2, lower1, upper1, upper2, tracer)
    ]
    port_shape = (20,) + TILE
    port, *loaded = call(
        port_kernel,
        [port_shape] + [tiles] * 5,
        arrays,
        in_specs=[hbm] * 5,
        scratch=[pltpu.SemaphoreType.DMA((5, CHUNKS))],
        name="segment_port",
    )
    chip, core_split = call(
        core_kernel, [port_shape] * 2, [port, exchange(port, 1, 1)], name="core_join"
    )
    by_x = [exchange(chip, k, 8) for k in (2, 4, 6)]
    (spikes,) = call(
        spikes_kernel,
        [(5, ROWS) + TILE],
        loaded + [chip],
        scratch=[pltpu.VMEM((ROWS,) + TILE, jnp.float32)] * 2,
        name="segment_spikes",
    )
    group, pair_x, top_x = call(group_kernel, [port_shape] * 3, [chip] + by_x, name="x_join")
    by_y = [exchange(group, k, 2) for k in (8, 16, 24)]
    low_ends, high_ends = call(
        solve_kernel,
        [(4,) + TILE] * 2,
        [group] + by_y + [top_x, pair_x, core_split, spikes],
        name="y_solve",
    )
    (out,) = call(
        combine_kernel,
        [tiles],
        [exchange(low_ends, 1, 1), high_ends, spikes],
        out_specs=[hbm],
        scratch=[pltpu.VMEM(tiles, jnp.float32), pltpu.SemaphoreType.DMA((SUBS,))],
        name="combine",
    )
    return out.reshape(16, 8, 8, 128).transpose(0, 2, 1, 3).reshape(ROWS, 1024)


def solution(mesh):
    spec = P("lon", "lat")
    return jax.shard_map(
        per_device, mesh=mesh, in_specs=(spec,) * 5, out_specs=spec, check_vma=False
    )
```

```python
import jax
import jax.numpy as jnp
from jax import lax
from jax.experimental import pallas as pl
from jax.experimental.pallas import tpu as pltpu
from jax.sharding import PartitionSpec as P

ROWS = 128
SUBS = 2
CHUNKS = 8
WRITES = 4
TILE = (8, 128)
VMEM_BYTES = 12 << 20


def eliminate(state, coefs):
    (far_g, far_a, far_b, far_p, far_q), (near_g, near_a, near_b, near_p, near_q) = state
    low2, low1, up1, up2, target = coefs
    minus_diag = (((low2 + low1) + up1) + up2) - 1.0
    beta = low1 + low2 * far_p
    scale = pl.reciprocal(minus_diag - low2 * far_q - beta * near_p)
    new_g = (low2 * far_g + beta * near_g - target) * scale
    new_a = (low2 * far_a + beta * near_a) * scale
    new_b = (low2 * far_b + beta * near_b) * scale
    new_p = (up1 + beta * near_q) * scale
    new_q = up2 * scale
    return (new_g, new_a, new_b, new_p, new_q)


def eliminate_first(coefs):
    low2, low1, up1, up2, target = coefs
    scale = pl.reciprocal((((low2 + low1) + up1) + up2) - 1.0)
    return (-target * scale, low2 * scale, low1 * scale, up1 * scale, up2 * scale)


def eliminate_second(first, coefs):
    near_g, near_a, near_b, near_p, near_q = first
    low2, low1, up1, up2, target = coefs
    scale = pl.reciprocal((((low2 + low1) + up1) + up2) - 1.0 - low1 * near_p)
    return (
        (low1 * near_g - target) * scale,
        low1 * near_a * scale,
        (low2 + low1 * near_b) * scale,
        (up1 + low1 * near_q) * scale,
        up2 * scale,
    )


def carry_on(head, row):
    g, a, b, p, q = head
    row_g, row_a, row_b, row_p, row_q = row
    return (g + p * row_g, a + p * row_a, b + p * row_b, q + p * row_p, p * row_q)


def affine(row, w, e):
    return row[0] + row[1] * w[0] + row[2] * w[1] + row[3] * e[0] + row[4] * e[1]


def mix(row, left, right):
    return tuple(row[0] * x + row[1] * y for x, y in zip(left, right))


def split_of(first, second):
    r0, r1 = first[2], first[3]
    l0, l1 = second[0], second[1]
    n00 = r0[3] * l0[1] + r0[4] * l1[1]
    n01 = r0[3] * l0[2] + r0[4] * l1[2]
    n10 = r1[3] * l0[1] + r1[4] * l1[1]
    n11 = r1[3] * l0[2] + r1[4] * l1[2]
    d00 = 1.0 - n00
    d11 = 1.0 - n11
    inv = pl.reciprocal(d00 * d11 - n01 * n10)
    k0 = (d11 * inv, n01 * inv)
    k1 = (n10 * inv, d00 * inv)
    s0 = (r0[0] + r0[3] * l0[0] + r0[4] * l1[0], r0[1], r0[2]) + mix(r0[3:5], l0[3:5], l1[3:5])
    s1 = (r1[0] + r1[3] * l0[0] + r1[4] * l1[0], r1[1], r1[2]) + mix(r1[3:5], l0[3:5], l1[3:5])
    a0 = mix(k0, s0, s1)
    a1 = mix(k1, s0, s1)
    b0 = mix(l0[1:3], a0, a1)
    b1 = mix(l1[1:3], a0, a1)
    b0 = (b0[0] + l0[0], b0[1], b0[2], b0[3] + l0[3], b0[4] + l0[4])
    b1 = (b1[0] + l1[0], b1[1], b1[2], b1[3] + l1[3], b1[4] + l1[4])
    return (a0, a1, b0, b1)


def join(first, second, split):
    a0, a1, b0, b1 = split
    left, right = [], []
    for row in first[0:2]:
        far = mix(row[3:5], b0, b1)
        left.append((row[0] + far[0], row[1] + far[1], row[2] + far[2], far[3], far[4]))
    for row in second[2:4]:
        far = mix(row[1:3], a0, a1)
        right.append((row[0] + far[0], far[1], far[2], row[3] + far[3], row[4] + far[4]))
    return tuple(left + right)


def read_port(ref):
    return tuple(tuple(ref[5 * i + j] for j in range(5)) for i in range(4))


def write_port(ref, port):
    for i in range(4):
        for j in range(5):
            ref[5 * i + j] = port[i][j]


def swap_if(flag, one, two):
    first = tuple(tuple(jnp.where(flag, y, x) for x, y in zip(u, v)) for u, v in zip(one, two))
    second = tuple(tuple(jnp.where(flag, x, y) for x, y in zip(u, v)) for u, v in zip(one, two))
    return first, second


def row_of(buffers, sub, chunk, step):
    return tuple(buf[sub, chunk, pl.ds(step, 8, stride=8), :] for buf in buffers)


def place_of(i):
    block, step = divmod(i, 8)
    return block // CHUNKS, block % CHUNKS, step


def port_kernel(*refs):
    sources, out, buffers, sems = refs[0:5], refs[5], refs[6:11], refs[11]
    copies = [
        [
            pltpu.make_async_copy(src.at[:, c], buf.at[:, c], sems.at[i, c])
            for i, (src, buf) in enumerate(zip(sources, buffers))
        ]
        for c in range(CHUNKS)
    ]
    for group in copies:
        for copy in group:
            copy.start()
    far, near = [None] * SUBS, [None] * SUBS
    head0, head1 = [None] * SUBS, [None] * SUBS
    for c in range(CHUNKS):
        for copy in copies[c]:
            copy.wait()
        for step in range(8):
            for s in range(SUBS):
                coefs = row_of(buffers, s, c, step)
                if c == 0 and step == 0:
                    near[s] = eliminate_first(coefs)
                    head0[s] = near[s]
                    continue
                if c == 0 and step == 1:
                    row = eliminate_second(near[s], coefs)
                    head1[s] = row
                else:
                    row = eliminate((far[s], near[s]), coefs)
                    head1[s] = carry_on(head1[s], row)
                head0[s] = carry_on(head0[s], row)
                far[s], near[s] = near[s], row
    ports = []
    for s in range(SUBS):
        g, a, b, p, q = far[s]
        row = near[s]
        tail0 = (g + p * row[0], a + p * row[1], b + p * row[2], q + p * row[3], p * row[4])
        ports.append((head0[s], head1[s], tail0, row))
    while len(ports) > 1:
        ports = [
            join(ports[i], ports[i + 1], split_of(ports[i], ports[i + 1]))
            for i in range(0, len(ports), 2)
        ]
    write_port(out, ports[0])


def spikes_kernel(l2, l1, u1, u2, tr, after, out, p_buf, q_buf):
    buffers = (l2, l1, u1, u2, tr)
    far, near = None, None
    for i in range(ROWS):
        coefs = row_of(buffers, *place_of(i))
        if i == 0:
            row = eliminate_first(coefs)
        elif i == 1:
            row = eliminate_second(near, coefs)
        else:
            row = eliminate((far, near), coefs)
        out[0, i], out[1, i], out[2, i] = row[0], row[1], row[2]
        p_buf[i], q_buf[i] = row[3], row[4]
        far, near = near, row
    zero = jnp.zeros(TILE, jnp.float32)
    one = jnp.ones(TILE, jnp.float32)
    next1 = (zero, zero, zero, one, zero)
    next2 = (zero, zero, zero, zero, one)
    for i in reversed(range(ROWS)):
        p, q = p_buf[i], q_buf[i]
        own = mix((p, q), next1, next2)
        own = (own[0] + out[0, i], own[1] + out[1, i], own[2] + out[2, i], own[3], own[4])
        (target,) = row_of((tr,), *place_of(i))
        out[0, i] = own[0] + own[0] - target
        for k in range(1, 5):
            out[k, i] = own[k]
        next2 = next1
        next1 = own


def core_kernel(own_ref, other_ref, out, split_out):
    is_high = lax.axis_index("lon") % 2 == 1
    first, second = swap_if(is_high, read_port(own_ref), read_port(other_ref))
    split = split_of(first, second)
    write_port(split_out, split)
    write_port(out, join(first, second, split))


def bits(divisor):
    place = (lax.axis_index("lon") // divisor) % 4
    return place % 2 == 1, place // 2 == 1


def group_kernel(own_ref, by1, by2, by3, out, split_pair, split_top):
    low_bit, high_bit = bits(2)
    first, second = swap_if(low_bit, read_port(own_ref), read_port(by1))
    split = split_of(first, second)
    write_port(split_pair, split)
    mine = join(first, second, split)
    first, second = swap_if(low_bit, read_port(by2), read_port(by3))
    theirs = join(first, second, split_of(first, second))
    first, second = swap_if(high_bit, mine, theirs)
    split = split_of(first, second)
    write_port(split_top, split)
    write_port(out, join(first, second, split))


def descend(flag, split, w, e):
    a0, a1 = affine(split[0], w, e), affine(split[1], w, e)
    b0, b1 = affine(split[2], w, e), affine(split[3], w, e)
    new_w = (jnp.where(flag, a0, w[0]), jnp.where(flag, a1, w[1]))
    new_e = (jnp.where(flag, e[0], b0), jnp.where(flag, e[1], b1))
    return new_w, new_e


def solve_kernel(own_ref, by1, by2, by3, top_x, pair_x, core, before, low_out, high_out):
    low_bit, high_bit = bits(8)
    first, second = swap_if(low_bit, read_port(own_ref), read_port(by1))
    split_mine = split_of(first, second)
    mine = join(first, second, split_mine)
    first, second = swap_if(low_bit, read_port(by2), read_port(by3))
    theirs = join(first, second, split_of(first, second))
    first, second = swap_if(high_bit, mine, theirs)
    zero = jnp.zeros(TILE, jnp.float32)
    w, e = (zero, zero), (zero, zero)
    w, e = descend(high_bit, split_of(first, second), w, e)
    w, e = descend(low_bit, split_mine, w, e)
    low_bit, high_bit = bits(2)
    w, e = descend(high_bit, read_port(top_x), w, e)
    w, e = descend(low_bit, read_port(pair_x), w, e)
    a0, a1, b0, b1 = (affine(row, w, e) for row in read_port(core))
    for k, value in enumerate((w[0], w[1], b0, b1)):
        low_out[k] = value + value
    for k, value in enumerate((a0, a1, e[0], e[1])):
        high_out[k] = value + value


def combine_kernel(received, high_own, spikes, out, stage, sems):
    is_high = lax.axis_index("lon") % 2 == 1
    weights = [jnp.where(is_high, high_own[k], received[k]) for k in range(4)]
    copies = []
    size = ROWS // 8 // WRITES
    for piece in range(WRITES):
        for block in range(piece * size, (piece + 1) * size):
            for step in range(8):
                i = 8 * block + step
                value = spikes[0, i]
                for k in range(4):
                    value = value + spikes[k + 1, i] * weights[k]
                stage[block, pl.ds(step, 8, stride=8), :] = value
        span = pl.ds(piece * size, size)
        copy = pltpu.make_async_copy(stage.at[span], out.at[span], sems.at[piece])
        copy.start()
        copies.append(copy)
    for copy in copies:
        copy.wait()


def call(kernel, outs, operands, out_specs=None, in_specs=None, scratch=(), name=None):
    vmem = pl.BlockSpec(memory_space=pltpu.VMEM)
    return pl.pallas_call(
        kernel,
        out_shape=[jax.ShapeDtypeStruct(shape, jnp.float32) for shape in outs],
        in_specs=in_specs or [vmem] * len(operands),
        out_specs=out_specs or [vmem] * len(outs),
        scratch_shapes=list(scratch),
        compiler_params=pltpu.CompilerParams(vmem_limit_bytes=VMEM_BYTES),
        name=name,
    )(*operands)


def exchange(port, odd_mask, even_mask):
    pairs = [(i, i ^ (odd_mask if i % 2 else even_mask)) for i in range(32)]
    return lax.ppermute(port, "lon", pairs)


def per_device(tracer, lower2, lower1, upper1, upper2):
    vmem = pl.BlockSpec(memory_space=pltpu.VMEM)
    hbm = pl.BlockSpec(memory_space=pltpu.HBM)
    tiles = (SUBS, CHUNKS, 64, 128)
    blocks = (SUBS * CHUNKS, 64, 128)

    def view(array):
        return array.reshape(16, 8, 8, 128).transpose(0, 2, 1, 3).reshape(tiles)

    arrays = [
        pltpu.with_memory_space_constraint(view(a), pltpu.HBM)
        for a in (lower2, lower1, upper1, upper2, tracer)
    ]
    port_shape = (20,) + TILE
    port, *loaded = call(
        port_kernel,
        [port_shape] + [tiles] * 5,
        arrays,
        in_specs=[hbm] * 5,
        scratch=[pltpu.SemaphoreType.DMA((5, CHUNKS))],
        name="segment_port",
    )
    chip, core_split = call(
        core_kernel, [port_shape] * 2, [port, exchange(port, 1, 1)], name="core_join"
    )
    by_x = [exchange(chip, k, 8) for k in (2, 4, 6)]
    (spikes,) = call(
        spikes_kernel,
        [(5, ROWS) + TILE],
        loaded + [chip],
        scratch=[pltpu.VMEM((ROWS,) + TILE, jnp.float32)] * 2,
        name="segment_spikes",
    )
    group, pair_x, top_x = call(group_kernel, [port_shape] * 3, [chip] + by_x, name="x_join")
    by_y = [exchange(group, k, 2) for k in (8, 16, 24)]
    low_ends, high_ends = call(
        solve_kernel,
        [(4,) + TILE] * 2,
        [group] + by_y + [top_x, pair_x, core_split, spikes],
        name="y_solve",
    )
    (out,) = call(
        combine_kernel,
        [blocks],
        [exchange(low_ends, 1, 1), high_ends, spikes],
        out_specs=[hbm],
        scratch=[pltpu.VMEM(blocks, jnp.float32), pltpu.SemaphoreType.DMA((WRITES,))],
        name="combine",
    )
    return out.reshape(16, 8, 8, 128).transpose(0, 2, 1, 3).reshape(ROWS, 1024)


def solution(mesh):
    spec = P("lon", "lat")
    return jax.shard_map(
        per_device, mesh=mesh, in_specs=(spec,) * 5, out_specs=spec, check_vma=False
    )
```

```python
import jax
import jax.numpy as jnp
from jax import lax
from jax.experimental import pallas as pl
from jax.experimental.pallas import tpu as pltpu
from jax.sharding import PartitionSpec as P

ROWS = 128
SUBS = 2
CHUNKS = 8
WRITES = 4
TILE = (8, 128)
VMEM_BYTES = 12 << 20


def eliminate(state, coefs):
    (far_g, far_a, far_b, far_p, far_q), (near_g, near_a, near_b, near_p, near_q) = state
    low2, low1, up1, up2, target = coefs
    minus_diag = (((low2 + low1) + up1) + up2) - 1.0
    beta = low1 + low2 * far_p
    scale = pl.reciprocal(minus_diag - low2 * far_q - beta * near_p)
    new_g = (low2 * far_g + beta * near_g - target) * scale
    new_a = (low2 * far_a + beta * near_a) * scale
    new_b = (low2 * far_b + beta * near_b) * scale
    new_p = (up1 + beta * near_q) * scale
    new_q = up2 * scale
    return (new_g, new_a, new_b, new_p, new_q)


def eliminate_first(coefs):
    low2, low1, up1, up2, target = coefs
    scale = pl.reciprocal((((low2 + low1) + up1) + up2) - 1.0)
    return (-target * scale, low2 * scale, low1 * scale, up1 * scale, up2 * scale)


def eliminate_second(first, coefs):
    near_g, near_a, near_b, near_p, near_q = first
    low2, low1, up1, up2, target = coefs
    scale = pl.reciprocal((((low2 + low1) + up1) + up2) - 1.0 - low1 * near_p)
    return (
        (low1 * near_g - target) * scale,
        low1 * near_a * scale,
        (low2 + low1 * near_b) * scale,
        (up1 + low1 * near_q) * scale,
        up2 * scale,
    )


def carry_on(head, row):
    g, a, b, p, q = head
    row_g, row_a, row_b, row_p, row_q = row
    return (g + p * row_g, a + p * row_a, b + p * row_b, q + p * row_p, p * row_q)


def affine(row, w, e):
    return row[0] + row[1] * w[0] + row[2] * w[1] + row[3] * e[0] + row[4] * e[1]


def mix(row, left, right):
    return tuple(row[0] * x + row[1] * y for x, y in zip(left, right))


def split_of(first, second):
    r0, r1 = first[2], first[3]
    l0, l1 = second[0], second[1]
    n00 = r0[3] * l0[1] + r0[4] * l1[1]
    n01 = r0[3] * l0[2] + r0[4] * l1[2]
    n10 = r1[3] * l0[1] + r1[4] * l1[1]
    n11 = r1[3] * l0[2] + r1[4] * l1[2]
    d00 = 1.0 - n00
    d11 = 1.0 - n11
    inv = pl.reciprocal(d00 * d11 - n01 * n10)
    k0 = (d11 * inv, n01 * inv)
    k1 = (n10 * inv, d00 * inv)
    s0 = (r0[0] + r0[3] * l0[0] + r0[4] * l1[0], r0[1], r0[2]) + mix(r0[3:5], l0[3:5], l1[3:5])
    s1 = (r1[0] + r1[3] * l0[0] + r1[4] * l1[0], r1[1], r1[2]) + mix(r1[3:5], l0[3:5], l1[3:5])
    a0 = mix(k0, s0, s1)
    a1 = mix(k1, s0, s1)
    b0 = mix(l0[1:3], a0, a1)
    b1 = mix(l1[1:3], a0, a1)
    b0 = (b0[0] + l0[0], b0[1], b0[2], b0[3] + l0[3], b0[4] + l0[4])
    b1 = (b1[0] + l1[0], b1[1], b1[2], b1[3] + l1[3], b1[4] + l1[4])
    return (a0, a1, b0, b1)


def join(first, second, split):
    a0, a1, b0, b1 = split
    left, right = [], []
    for row in first[0:2]:
        far = mix(row[3:5], b0, b1)
        left.append((row[0] + far[0], row[1] + far[1], row[2] + far[2], far[3], far[4]))
    for row in second[2:4]:
        far = mix(row[1:3], a0, a1)
        right.append((row[0] + far[0], far[1], far[2], row[3] + far[3], row[4] + far[4]))
    return tuple(left + right)


def read_port(ref):
    return tuple(tuple(ref[5 * i + j] for j in range(5)) for i in range(4))


def write_port(ref, port):
    for i in range(4):
        for j in range(5):
            ref[5 * i + j] = port[i][j]


def swap_if(flag, one, two):
    first = tuple(tuple(jnp.where(flag, y, x) for x, y in zip(u, v)) for u, v in zip(one, two))
    second = tuple(tuple(jnp.where(flag, x, y) for x, y in zip(u, v)) for u, v in zip(one, two))
    return first, second


def row_of(buffers, sub, chunk, step):
    return tuple(buf[sub, chunk, pl.ds(step, 8, stride=8), :] for buf in buffers)


def place_of(i):
    block, step = divmod(i, 8)
    return block // CHUNKS, block % CHUNKS, step


def port_kernel(*refs):
    sources, out, buffers, sems = refs[0:5], refs[5], refs[6:11], refs[11]
    copies = [
        [
            pltpu.make_async_copy(src.at[:, c], buf.at[:, c], sems.at[i, c])
            for i, (src, buf) in enumerate(zip(sources, buffers))
        ]
        for c in range(CHUNKS)
    ]
    for group in copies:
        for copy in group:
            copy.start()
    far, near = [None] * SUBS, [None] * SUBS
    head0, head1 = [None] * SUBS, [None] * SUBS
    for c in range(CHUNKS):
        for copy in copies[c]:
            copy.wait()
        for step in range(8):
            for s in range(SUBS):
                coefs = row_of(buffers, s, c, step)
                if c == 0 and step == 0:
                    near[s] = eliminate_first(coefs)
                    head0[s] = near[s]
                    continue
                if c == 0 and step == 1:
                    row = eliminate_second(near[s], coefs)
                    head1[s] = row
                else:
                    row = eliminate((far[s], near[s]), coefs)
                    head1[s] = carry_on(head1[s], row)
                head0[s] = carry_on(head0[s], row)
                far[s], near[s] = near[s], row
    ports = []
    for s in range(SUBS):
        g, a, b, p, q = far[s]
        row = near[s]
        tail0 = (g + p * row[0], a + p * row[1], b + p * row[2], q + p * row[3], p * row[4])
        ports.append((head0[s], head1[s], tail0, row))
    while len(ports) > 1:
        ports = [
            join(ports[i], ports[i + 1], split_of(ports[i], ports[i + 1]))
            for i in range(0, len(ports), 2)
        ]
    write_port(out, ports[0])


def spikes_kernel(l2, l1, u1, u2, tr, after, out, p_buf, q_buf):
    buffers = (l2, l1, u1, u2, tr)
    far, near = None, None
    for i in range(ROWS):
        coefs = row_of(buffers, *place_of(i))
        if i == 0:
            row = eliminate_first(coefs)
        elif i == 1:
            row = eliminate_second(near, coefs)
        else:
            row = eliminate((far, near), coefs)
        out[0, i], out[1, i], out[2, i] = row[0], row[1], row[2]
        p_buf[i], q_buf[i] = row[3], row[4]
        far, near = near, row
    zero = jnp.zeros(TILE, jnp.float32)
    one = jnp.ones(TILE, jnp.float32)
    next1 = (zero, zero, zero, one, zero)
    next2 = (zero, zero, zero, zero, one)
    for i in reversed(range(ROWS)):
        p, q = p_buf[i], q_buf[i]
        own = mix((p, q), next1, next2)
        own = (own[0] + out[0, i], own[1] + out[1, i], own[2] + out[2, i], own[3], own[4])
        (target,) = row_of((tr,), *place_of(i))
        out[0, i] = own[0] + own[0] - target
        for k in range(1, 5):
            out[k, i] = own[k]
        next2 = next1
        next1 = own


def core_kernel(own_ref, other_ref, out, split_out):
    is_high = lax.axis_index("lon") % 2 == 1
    first, second = swap_if(is_high, read_port(own_ref), read_port(other_ref))
    split = split_of(first, second)
    write_port(split_out, split)
    write_port(out, join(first, second, split))


def bits(divisor):
    place = (lax.axis_index("lon") // divisor) % 4
    return place % 2 == 1, place // 2 == 1


def group_kernel(own_ref, by1, by2, by3, out, split_pair, split_top):
    low_bit, high_bit = bits(2)
    first, second = swap_if(low_bit, read_port(own_ref), read_port(by1))
    split = split_of(first, second)
    write_port(split_pair, split)
    mine = join(first, second, split)
    first, second = swap_if(low_bit, read_port(by2), read_port(by3))
    theirs = join(first, second, split_of(first, second))
    first, second = swap_if(high_bit, mine, theirs)
    split = split_of(first, second)
    write_port(split_top, split)
    write_port(out, join(first, second, split))


def descend(flag, split, w, e):
    a0, a1 = affine(split[0], w, e), affine(split[1], w, e)
    b0, b1 = affine(split[2], w, e), affine(split[3], w, e)
    new_w = (jnp.where(flag, a0, w[0]), jnp.where(flag, a1, w[1]))
    new_e = (jnp.where(flag, e[0], b0), jnp.where(flag, e[1], b1))
    return new_w, new_e


def solve_kernel(own_ref, by1, by2, by3, top_x, pair_x, core, before, low_out, high_out):
    low_bit, high_bit = bits(8)
    first, second = swap_if(low_bit, read_port(own_ref), read_port(by1))
    split_mine = split_of(first, second)
    mine = join(first, second, split_mine)
    first, second = swap_if(low_bit, read_port(by2), read_port(by3))
    theirs = join(first, second, split_of(first, second))
    first, second = swap_if(high_bit, mine, theirs)
    zero = jnp.zeros(TILE, jnp.float32)
    w, e = (zero, zero), (zero, zero)
    w, e = descend(high_bit, split_of(first, second), w, e)
    w, e = descend(low_bit, split_mine, w, e)
    low_bit, high_bit = bits(2)
    w, e = descend(high_bit, read_port(top_x), w, e)
    w, e = descend(low_bit, read_port(pair_x), w, e)
    a0, a1, b0, b1 = (affine(row, w, e) for row in read_port(core))
    for k, value in enumerate((w[0], w[1], b0, b1)):
        low_out[k] = value + value
    for k, value in enumerate((a0, a1, e[0], e[1])):
        high_out[k] = value + value


def combine(ends, spikes, out, stage, sems):
    weights = [ends[k] for k in range(4)]
    copies = []
    size = ROWS // 8 // WRITES
    for piece in range(WRITES):
        for block in range(piece * size, (piece + 1) * size):
            for step in range(8):
                i = 8 * block + step
                value = spikes[0, i]
                for k in range(4):
                    value = value + spikes[k + 1, i] * weights[k]
                stage[block, pl.ds(step, 8, stride=8), :] = value
        span = pl.ds(piece * size, size)
        copy = pltpu.make_async_copy(stage.at[span], out.at[span], sems.at[piece])
        copy.start()
        copies.append(copy)
    for copy in copies:
        copy.wait()


def combine_odd_kernel(ends, spikes, out, stage, sems):
    @pl.when(lax.axis_index("lon") % 2 == 1)
    def _():
        combine(ends, spikes, out, stage, sems)


def combine_even_kernel(ends, spikes, partial, out, stage, sems):
    @pl.when(lax.axis_index("lon") % 2 == 0)
    def _():
        combine(ends, spikes, out, stage, sems)


def call(
    kernel, outs, operands, out_specs=None, in_specs=None, scratch=(), name=None, aliases={}
):
    vmem = pl.BlockSpec(memory_space=pltpu.VMEM)
    return pl.pallas_call(
        kernel,
        out_shape=[jax.ShapeDtypeStruct(shape, jnp.float32) for shape in outs],
        in_specs=in_specs or [vmem] * len(operands),
        out_specs=out_specs or [vmem] * len(outs),
        scratch_shapes=list(scratch),
        compiler_params=pltpu.CompilerParams(vmem_limit_bytes=VMEM_BYTES),
        input_output_aliases=aliases,
        name=name,
    )(*operands)


def exchange(port, odd_mask, even_mask):
    pairs = [(i, i ^ (odd_mask if i % 2 else even_mask)) for i in range(32)]
    return lax.ppermute(port, "lon", pairs)


def per_device(tracer, lower2, lower1, upper1, upper2):
    vmem = pl.BlockSpec(memory_space=pltpu.VMEM)
    hbm = pl.BlockSpec(memory_space=pltpu.HBM)
    tiles = (SUBS, CHUNKS, 64, 128)
    blocks = (SUBS * CHUNKS, 64, 128)

    def view(array):
        return array.reshape(16, 8, 8, 128).transpose(0, 2, 1, 3).reshape(tiles)

    arrays = [
        pltpu.with_memory_space_constraint(view(a), pltpu.HBM)
        for a in (lower2, lower1, upper1, upper2, tracer)
    ]
    port_shape = (20,) + TILE
    port, *loaded = call(
        port_kernel,
        [port_shape] + [tiles] * 5,
        arrays,
        in_specs=[hbm] * 5,
        scratch=[pltpu.SemaphoreType.DMA((5, CHUNKS))],
        name="segment_port",
    )
    chip, core_split = call(
        core_kernel, [port_shape] * 2, [port, exchange(port, 1, 1)], name="core_join"
    )
    by_x = [exchange(chip, k, 8) for k in (2, 4, 6)]
    (spikes,) = call(
        spikes_kernel,
        [(5, ROWS) + TILE],
        loaded + [chip],
        scratch=[pltpu.VMEM((ROWS,) + TILE, jnp.float32)] * 2,
        name="segment_spikes",
    )
    group, pair_x, top_x = call(group_kernel, [port_shape] * 3, [chip] + by_x, name="x_join")
    by_y = [exchange(group, k, 2) for k in (8, 16, 24)]
    low_ends, high_ends = call(
        solve_kernel,
        [(4,) + TILE] * 2,
        [group] + by_y + [top_x, pair_x, core_split, spikes],
        name="y_solve",
    )
    received = exchange(low_ends, 1, 1)
    scratch = [pltpu.VMEM(blocks, jnp.float32), pltpu.SemaphoreType.DMA((WRITES,))]
    (out,) = call(
        combine_odd_kernel,
        [blocks],
        [high_ends, spikes],
        out_specs=[hbm],
        scratch=scratch,
        name="combine_odd",
    )
    (out,) = call(
        combine_even_kernel,
        [blocks],
        [received, spikes, out],
        in_specs=[vmem, vmem, hbm],
        out_specs=[hbm],
        scratch=scratch,
        name="combine_even",
        aliases={2: 0},
    )
    return out.reshape(16, 8, 8, 128).transpose(0, 2, 1, 3).reshape(ROWS, 1024)


def solution(mesh):
    spec = P("lon", "lat")
    return jax.shard_map(
        per_device, mesh=mesh, in_specs=(spec,) * 5, out_specs=spec, check_vma=False
    )
```

```python
import jax
import jax.numpy as jnp
from jax import lax
from jax.experimental import pallas as pl
from jax.experimental.pallas import tpu as pltpu
from jax.sharding import PartitionSpec as P

ROWS = 128
SUBS = 2
CHUNKS = 8
WRITES = 8
TILE = (8, 128)
VMEM_BYTES = 12 << 20


def eliminate(state, coefs):
    (far_g, far_a, far_b, far_p, far_q), (near_g, near_a, near_b, near_p, near_q) = state
    low2, low1, up1, up2, target = coefs
    minus_diag = (((low2 + low1) + up1) + up2) - 1.0
    beta = low1 + low2 * far_p
    scale = pl.reciprocal(minus_diag - low2 * far_q - beta * near_p)
    new_g = (low2 * far_g + beta * near_g - target) * scale
    new_a = (low2 * far_a + beta * near_a) * scale
    new_b = (low2 * far_b + beta * near_b) * scale
    new_p = (up1 + beta * near_q) * scale
    new_q = up2 * scale
    return (new_g, new_a, new_b, new_p, new_q)


def eliminate_first(coefs):
    low2, low1, up1, up2, target = coefs
    scale = pl.reciprocal((((low2 + low1) + up1) + up2) - 1.0)
    return (-target * scale, low2 * scale, low1 * scale, up1 * scale, up2 * scale)


def eliminate_second(first, coefs):
    near_g, near_a, near_b, near_p, near_q = first
    low2, low1, up1, up2, target = coefs
    scale = pl.reciprocal((((low2 + low1) + up1) + up2) - 1.0 - low1 * near_p)
    return (
        (low1 * near_g - target) * scale,
        low1 * near_a * scale,
        (low2 + low1 * near_b) * scale,
        (up1 + low1 * near_q) * scale,
        up2 * scale,
    )


def carry_on(head, row):
    g, a, b, p, q = head
    row_g, row_a, row_b, row_p, row_q = row
    return (g + p * row_g, a + p * row_a, b + p * row_b, q + p * row_p, p * row_q)


def affine(row, w, e):
    return row[0] + row[1] * w[0] + row[2] * w[1] + row[3] * e[0] + row[4] * e[1]


def mix(row, left, right):
    return tuple(row[0] * x + row[1] * y for x, y in zip(left, right))


def split_of(first, second):
    r0, r1 = first[2], first[3]
    l0, l1 = second[0], second[1]
    n00 = r0[3] * l0[1] + r0[4] * l1[1]
    n01 = r0[3] * l0[2] + r0[4] * l1[2]
    n10 = r1[3] * l0[1] + r1[4] * l1[1]
    n11 = r1[3] * l0[2] + r1[4] * l1[2]
    d00 = 1.0 - n00
    d11 = 1.0 - n11
    inv = pl.reciprocal(d00 * d11 - n01 * n10)
    k0 = (d11 * inv, n01 * inv)
    k1 = (n10 * inv, d00 * inv)
    s0 = (r0[0] + r0[3] * l0[0] + r0[4] * l1[0], r0[1], r0[2]) + mix(r0[3:5], l0[3:5], l1[3:5])
    s1 = (r1[0] + r1[3] * l0[0] + r1[4] * l1[0], r1[1], r1[2]) + mix(r1[3:5], l0[3:5], l1[3:5])
    a0 = mix(k0, s0, s1)
    a1 = mix(k1, s0, s1)
    b0 = mix(l0[1:3], a0, a1)
    b1 = mix(l1[1:3], a0, a1)
    b0 = (b0[0] + l0[0], b0[1], b0[2], b0[3] + l0[3], b0[4] + l0[4])
    b1 = (b1[0] + l1[0], b1[1], b1[2], b1[3] + l1[3], b1[4] + l1[4])
    return (a0, a1, b0, b1)


def join(first, second, split):
    a0, a1, b0, b1 = split
    left, right = [], []
    for row in first[0:2]:
        far = mix(row[3:5], b0, b1)
        left.append((row[0] + far[0], row[1] + far[1], row[2] + far[2], far[3], far[4]))
    for row in second[2:4]:
        far = mix(row[1:3], a0, a1)
        right.append((row[0] + far[0], far[1], far[2], row[3] + far[3], row[4] + far[4]))
    return tuple(left + right)


def read_port(ref):
    return tuple(tuple(ref[5 * i + j] for j in range(5)) for i in range(4))


def write_port(ref, port):
    for i in range(4):
        for j in range(5):
            ref[5 * i + j] = port[i][j]


def swap_if(flag, one, two):
    first = tuple(tuple(jnp.where(flag, y, x) for x, y in zip(u, v)) for u, v in zip(one, two))
    second = tuple(tuple(jnp.where(flag, x, y) for x, y in zip(u, v)) for u, v in zip(one, two))
    return first, second


def row_of(buffers, sub, chunk, step):
    return tuple(buf[sub, chunk, pl.ds(step, 8, stride=8), :] for buf in buffers)


def place_of(i):
    block, step = divmod(i, 8)
    return block // CHUNKS, block % CHUNKS, step


def port_kernel(*refs):
    sources, out, buffers, sems = refs[0:5], refs[5], refs[6:11], refs[11]
    copies = [
        [
            pltpu.make_async_copy(src.at[:, c], buf.at[:, c], sems.at[i, c])
            for i, (src, buf) in enumerate(zip(sources, buffers))
        ]
        for c in range(CHUNKS)
    ]
    for group in copies:
        for copy in group:
            copy.start()
    far, near = [None] * SUBS, [None] * SUBS
    head0, head1 = [None] * SUBS, [None] * SUBS
    for c in range(CHUNKS):
        for copy in copies[c]:
            copy.wait()
        for step in range(8):
            for s in range(SUBS):
                coefs = row_of(buffers, s, c, step)
                if c == 0 and step == 0:
                    near[s] = eliminate_first(coefs)
                    head0[s] = near[s]
                    continue
                if c == 0 and step == 1:
                    row = eliminate_second(near[s], coefs)
                    head1[s] = row
                else:
                    row = eliminate((far[s], near[s]), coefs)
                    head1[s] = carry_on(head1[s], row)
                head0[s] = carry_on(head0[s], row)
                far[s], near[s] = near[s], row
    ports = []
    for s in range(SUBS):
        g, a, b, p, q = far[s]
        row = near[s]
        tail0 = (g + p * row[0], a + p * row[1], b + p * row[2], q + p * row[3], p * row[4])
        ports.append((head0[s], head1[s], tail0, row))
    while len(ports) > 1:
        ports = [
            join(ports[i], ports[i + 1], split_of(ports[i], ports[i + 1]))
            for i in range(0, len(ports), 2)
        ]
    write_port(out, ports[0])


def spikes_kernel(l2, l1, u1, u2, tr, after, out, p_buf, q_buf):
    buffers = (l2, l1, u1, u2, tr)
    far, near = None, None
    for i in range(ROWS):
        coefs = row_of(buffers, *place_of(i))
        if i == 0:
            row = eliminate_first(coefs)
        elif i == 1:
            row = eliminate_second(near, coefs)
        else:
            row = eliminate((far, near), coefs)
        out[0, i], out[1, i], out[2, i] = row[0], row[1], row[2]
        p_buf[i], q_buf[i] = row[3], row[4]
        far, near = near, row
    zero = jnp.zeros(TILE, jnp.float32)
    one = jnp.ones(TILE, jnp.float32)
    next1 = (zero, zero, zero, one, zero)
    next2 = (zero, zero, zero, zero, one)
    for i in reversed(range(ROWS)):
        p, q = p_buf[i], q_buf[i]
        own = mix((p, q), next1, next2)
        own = (own[0] + out[0, i], own[1] + out[1, i], own[2] + out[2, i], own[3], own[4])
        (target,) = row_of((tr,), *place_of(i))
        out[0, i] = own[0] + own[0] - target
        for k in range(1, 5):
            out[k, i] = own[k]
        next2 = next1
        next1 = own


def core_kernel(own_ref, other_ref, out, split_out):
    is_high = lax.axis_index("lon") % 2 == 1
    first, second = swap_if(is_high, read_port(own_ref), read_port(other_ref))
    split = split_of(first, second)
    write_port(split_out, split)
    write_port(out, join(first, second, split))


def bits(divisor):
    place = (lax.axis_index("lon") // divisor) % 4
    return place % 2 == 1, place // 2 == 1


def group_kernel(own_ref, by1, by3, by2, out, split_pair, split_top):
    low_bit, high_bit = bits(2)
    first, second = swap_if(low_bit, read_port(own_ref), read_port(by1))
    split = split_of(first, second)
    write_port(split_pair, split)
    mine = join(first, second, split)
    first, second = swap_if(low_bit, read_port(by2), read_port(by3))
    theirs = join(first, second, split_of(first, second))
    first, second = swap_if(high_bit, mine, theirs)
    split = split_of(first, second)
    write_port(split_top, split)
    write_port(out, join(first, second, split))


def descend(flag, split, w, e):
    a0, a1 = affine(split[0], w, e), affine(split[1], w, e)
    b0, b1 = affine(split[2], w, e), affine(split[3], w, e)
    new_w = (jnp.where(flag, a0, w[0]), jnp.where(flag, a1, w[1]))
    new_e = (jnp.where(flag, e[0], b0), jnp.where(flag, e[1], b1))
    return new_w, new_e


def solve_kernel(own_ref, by1, by3, by2, top_x, pair_x, core, before, low_out, high_out):
    low_bit, high_bit = bits(8)
    first, second = swap_if(low_bit, read_port(own_ref), read_port(by1))
    split_mine = split_of(first, second)
    mine = join(first, second, split_mine)
    first, second = swap_if(low_bit, read_port(by2), read_port(by3))
    theirs = join(first, second, split_of(first, second))
    first, second = swap_if(high_bit, mine, theirs)
    zero = jnp.zeros(TILE, jnp.float32)
    w, e = (zero, zero), (zero, zero)
    w, e = descend(high_bit, split_of(first, second), w, e)
    w, e = descend(low_bit, split_mine, w, e)
    low_bit, high_bit = bits(2)
    w, e = descend(high_bit, read_port(top_x), w, e)
    w, e = descend(low_bit, read_port(pair_x), w, e)
    a0, a1, b0, b1 = (affine(row, w, e) for row in read_port(core))
    for k, value in enumerate((w[0], w[1], b0, b1)):
        low_out[k] = value + value
    for k, value in enumerate((a0, a1, e[0], e[1])):
        high_out[k] = value + value


def combine(ends, spikes, out, stage, sems):
    weights = [ends[k] for k in range(4)]
    copies = []
    size = ROWS // 8 // WRITES
    for piece in range(WRITES):
        for block in range(piece * size, (piece + 1) * size):
            for step in range(8):
                i = 8 * block + step
                value = spikes[0, i]
                for k in range(4):
                    value = value + spikes[k + 1, i] * weights[k]
                stage[block, pl.ds(step, 8, stride=8), :] = value
        span = pl.ds(piece * size, size)
        copy = pltpu.make_async_copy(stage.at[span], out.at[span], sems.at[piece])
        copy.start()
        copies.append(copy)
    for copy in copies:
        copy.wait()


def combine_odd_kernel(ends, spikes, out, stage, sems):
    @pl.when(lax.axis_index("lon") % 2 == 1)
    def _():
        combine(ends, spikes, out, stage, sems)


def combine_even_kernel(ends, spikes, partial, out, stage, sems):
    @pl.when(lax.axis_index("lon") % 2 == 0)
    def _():
        combine(ends, spikes, out, stage, sems)


def call(
    kernel, outs, operands, out_specs=None, in_specs=None, scratch=(), name=None, aliases={}
):
    vmem = pl.BlockSpec(memory_space=pltpu.VMEM)
    return pl.pallas_call(
        kernel,
        out_shape=[jax.ShapeDtypeStruct(shape, jnp.float32) for shape in outs],
        in_specs=in_specs or [vmem] * len(operands),
        out_specs=out_specs or [vmem] * len(outs),
        scratch_shapes=list(scratch),
        compiler_params=pltpu.CompilerParams(vmem_limit_bytes=VMEM_BYTES),
        input_output_aliases=aliases,
        name=name,
    )(*operands)


def exchange(port, odd_mask, even_mask):
    pairs = [(i, i ^ (odd_mask if i % 2 else even_mask)) for i in range(32)]
    return lax.ppermute(port, "lon", pairs)


def per_device(tracer, lower2, lower1, upper1, upper2):
    vmem = pl.BlockSpec(memory_space=pltpu.VMEM)
    hbm = pl.BlockSpec(memory_space=pltpu.HBM)
    tiles = (SUBS, CHUNKS, 64, 128)
    blocks = (SUBS * CHUNKS, 64, 128)

    def view(array):
        return array.reshape(16, 8, 8, 128).transpose(0, 2, 1, 3).reshape(tiles)

    arrays = [
        pltpu.with_memory_space_constraint(view(a), pltpu.HBM)
        for a in (lower2, lower1, upper1, upper2, tracer)
    ]
    port_shape = (20,) + TILE
    port, *loaded = call(
        port_kernel,
        [port_shape] + [tiles] * 5,
        arrays,
        in_specs=[hbm] * 5,
        scratch=[pltpu.SemaphoreType.DMA((5, CHUNKS))],
        name="segment_port",
    )
    chip, core_split = call(
        core_kernel, [port_shape] * 2, [port, exchange(port, 1, 1)], name="core_join"
    )
    x_near, x_end, x_far = (exchange(chip, k, 8) for k in (2, 6, 4))
    (spikes,) = call(
        spikes_kernel,
        [(5, ROWS) + TILE],
        loaded + [chip],
        scratch=[pltpu.VMEM((ROWS,) + TILE, jnp.float32)] * 2,
        name="segment_spikes",
    )
    group, pair_x, top_x = call(group_kernel, [port_shape] * 3, [chip, x_near, x_end, x_far], name="x_join")
    y_near, y_end, y_far = (exchange(group, k, 2) for k in (8, 24, 16))
    low_ends, high_ends = call(
        solve_kernel,
        [(4,) + TILE] * 2,
        [group, y_near, y_end, y_far, top_x, pair_x, core_split, spikes],
        name="y_solve",
    )
    received = exchange(low_ends, 1, 1)
    scratch = [pltpu.VMEM(blocks, jnp.float32), pltpu.SemaphoreType.DMA((WRITES,))]
    (out,) = call(
        combine_odd_kernel,
        [blocks],
        [high_ends, spikes],
        out_specs=[hbm],
        scratch=scratch,
        name="combine_odd",
    )
    (out,) = call(
        combine_even_kernel,
        [blocks],
        [received, spikes, out],
        in_specs=[vmem, vmem, hbm],
        out_specs=[hbm],
        scratch=scratch,
        name="combine_even",
        aliases={2: 0},
    )
    return out.reshape(16, 8, 8, 128).transpose(0, 2, 1, 3).reshape(ROWS, 1024)


def solution(mesh):
    spec = P("lon", "lat")
    return jax.shard_map(
        per_device, mesh=mesh, in_specs=(spec,) * 5, out_specs=spec, check_vma=False
    )
```

```python
import jax
import jax.numpy as jnp
from jax import lax
from jax.experimental import pallas as pl
from jax.experimental.pallas import tpu as pltpu
from jax.sharding import PartitionSpec as P

ROWS = 128
SUBS = 2
CHUNKS = 8
WRITES = 8
TILE = (8, 128)
VMEM_BYTES = 12 << 20


def eliminate(state, coefs):
    (far_g, far_a, far_b, far_p, far_q), (near_g, near_a, near_b, near_p, near_q) = state
    low2, low1, up1, up2, target = coefs
    minus_diag = (((low2 + low1) + up1) + up2) - 1.0
    beta = low1 + low2 * far_p
    scale = pl.reciprocal(minus_diag - low2 * far_q - beta * near_p)
    new_g = (low2 * far_g + beta * near_g - target) * scale
    new_a = (low2 * far_a + beta * near_a) * scale
    new_b = (low2 * far_b + beta * near_b) * scale
    new_p = (up1 + beta * near_q) * scale
    new_q = up2 * scale
    return (new_g, new_a, new_b, new_p, new_q)


def eliminate_first(coefs):
    low2, low1, up1, up2, target = coefs
    scale = pl.reciprocal((((low2 + low1) + up1) + up2) - 1.0)
    return (-target * scale, low2 * scale, low1 * scale, up1 * scale, up2 * scale)


def eliminate_second(first, coefs):
    near_g, near_a, near_b, near_p, near_q = first
    low2, low1, up1, up2, target = coefs
    scale = pl.reciprocal((((low2 + low1) + up1) + up2) - 1.0 - low1 * near_p)
    return (
        (low1 * near_g - target) * scale,
        low1 * near_a * scale,
        (low2 + low1 * near_b) * scale,
        (up1 + low1 * near_q) * scale,
        up2 * scale,
    )


def carry_on(head, row):
    g, a, b, p, q = head
    row_g, row_a, row_b, row_p, row_q = row
    return (g + p * row_g, a + p * row_a, b + p * row_b, q + p * row_p, p * row_q)


def affine(row, w, e):
    return row[0] + row[1] * w[0] + row[2] * w[1] + row[3] * e[0] + row[4] * e[1]


def mix(row, left, right):
    return tuple(row[0] * x + row[1] * y for x, y in zip(left, right))


def split_of(first, second):
    r0, r1 = first[2], first[3]
    l0, l1 = second[0], second[1]
    n00 = r0[3] * l0[1] + r0[4] * l1[1]
    n01 = r0[3] * l0[2] + r0[4] * l1[2]
    n10 = r1[3] * l0[1] + r1[4] * l1[1]
    n11 = r1[3] * l0[2] + r1[4] * l1[2]
    d00 = 1.0 - n00
    d11 = 1.0 - n11
    inv = pl.reciprocal(d00 * d11 - n01 * n10)
    k0 = (d11 * inv, n01 * inv)
    k1 = (n10 * inv, d00 * inv)
    s0 = (r0[0] + r0[3] * l0[0] + r0[4] * l1[0], r0[1], r0[2]) + mix(r0[3:5], l0[3:5], l1[3:5])
    s1 = (r1[0] + r1[3] * l0[0] + r1[4] * l1[0], r1[1], r1[2]) + mix(r1[3:5], l0[3:5], l1[3:5])
    a0 = mix(k0, s0, s1)
    a1 = mix(k1, s0, s1)
    b0 = mix(l0[1:3], a0, a1)
    b1 = mix(l1[1:3], a0, a1)
    b0 = (b0[0] + l0[0], b0[1], b0[2], b0[3] + l0[3], b0[4] + l0[4])
    b1 = (b1[0] + l1[0], b1[1], b1[2], b1[3] + l1[3], b1[4] + l1[4])
    return (a0, a1, b0, b1)


def join(first, second, split):
    a0, a1, b0, b1 = split
    left, right = [], []
    for row in first[0:2]:
        far = mix(row[3:5], b0, b1)
        left.append((row[0] + far[0], row[1] + far[1], row[2] + far[2], far[3], far[4]))
    for row in second[2:4]:
        far = mix(row[1:3], a0, a1)
        right.append((row[0] + far[0], far[1], far[2], row[3] + far[3], row[4] + far[4]))
    return tuple(left + right)


def read_port(ref):
    return tuple(tuple(ref[5 * i + j] for j in range(5)) for i in range(4))


def write_port(ref, port):
    for i in range(4):
        for j in range(5):
            ref[5 * i + j] = port[i][j]


def swap_if(flag, one, two):
    first = tuple(tuple(jnp.where(flag, y, x) for x, y in zip(u, v)) for u, v in zip(one, two))
    second = tuple(tuple(jnp.where(flag, x, y) for x, y in zip(u, v)) for u, v in zip(one, two))
    return first, second


def row_of(buffers, sub, chunk, step):
    return tuple(buf[sub, chunk, pl.ds(step, 8, stride=8), :] for buf in buffers)


def place_of(i):
    block, step = divmod(i, 8)
    return block // CHUNKS, block % CHUNKS, step


def port_kernel(*refs):
    sources, out, buffers, sems = refs[0:5], refs[5], refs[6:11], refs[11]
    copies = [
        [
            pltpu.make_async_copy(src.at[:, c], buf.at[:, c], sems.at[i, c])
            for i, (src, buf) in enumerate(zip(sources, buffers))
        ]
        for c in range(CHUNKS)
    ]
    for group in copies:
        for copy in group:
            copy.start()
    far, near = [None] * SUBS, [None] * SUBS
    head0, head1 = [None] * SUBS, [None] * SUBS
    for c in range(CHUNKS):
        for copy in copies[c]:
            copy.wait()
        for step in range(8):
            for s in range(SUBS):
                coefs = row_of(buffers, s, c, step)
                if c == 0 and step == 0:
                    near[s] = eliminate_first(coefs)
                    head0[s] = near[s]
                    continue
                if c == 0 and step == 1:
                    row = eliminate_second(near[s], coefs)
                    head1[s] = row
                else:
                    row = eliminate((far[s], near[s]), coefs)
                    head1[s] = carry_on(head1[s], row)
                head0[s] = carry_on(head0[s], row)
                far[s], near[s] = near[s], row
    ports = []
    for s in range(SUBS):
        g, a, b, p, q = far[s]
        row = near[s]
        tail0 = (g + p * row[0], a + p * row[1], b + p * row[2], q + p * row[3], p * row[4])
        ports.append((head0[s], head1[s], tail0, row))
    while len(ports) > 1:
        ports = [
            join(ports[i], ports[i + 1], split_of(ports[i], ports[i + 1]))
            for i in range(0, len(ports), 2)
        ]
    write_port(out, ports[0])


def spikes_kernel(l2, l1, u1, u2, tr, after, out, p_buf, q_buf):
    buffers = (l2, l1, u1, u2, tr)
    far, near = None, None
    for i in range(ROWS):
        coefs = row_of(buffers, *place_of(i))
        if i == 0:
            row = eliminate_first(coefs)
        elif i == 1:
            row = eliminate_second(near, coefs)
        else:
            row = eliminate((far, near), coefs)
        out[0, i], out[1, i], out[2, i] = row[0], row[1], row[2]
        p_buf[i], q_buf[i] = row[3], row[4]
        far, near = near, row
    zero = jnp.zeros(TILE, jnp.float32)
    one = jnp.ones(TILE, jnp.float32)
    next1 = (zero, zero, zero, one, zero)
    next2 = (zero, zero, zero, zero, one)
    for i in reversed(range(ROWS)):
        p, q = p_buf[i], q_buf[i]
        own = mix((p, q), next1, next2)
        own = (own[0] + out[0, i], own[1] + out[1, i], own[2] + out[2, i], own[3], own[4])
        (target,) = row_of((tr,), *place_of(i))
        out[0, i] = own[0] + own[0] - target
        for k in range(1, 5):
            out[k, i] = own[k]
        next2 = next1
        next1 = own


def core_kernel(own_ref, other_ref, out, split_out):
    is_high = lax.axis_index("lon") % 2 == 1
    first, second = swap_if(is_high, read_port(own_ref), read_port(other_ref))
    split = split_of(first, second)
    write_port(split_out, split)
    write_port(out, join(first, second, split))


def bits(divisor):
    place = (lax.axis_index("lon") // divisor) % 4
    return place % 2 == 1, place // 2 == 1


def group_kernel(own_ref, by1, by3, by2, out, split_pair, split_top):
    low_bit, high_bit = bits(2)
    first, second = swap_if(low_bit, read_port(own_ref), read_port(by1))
    split = split_of(first, second)
    write_port(split_pair, split)
    mine = join(first, second, split)
    first, second = swap_if(low_bit, read_port(by2), read_port(by3))
    theirs = join(first, second, split_of(first, second))
    first, second = swap_if(high_bit, mine, theirs)
    split = split_of(first, second)
    write_port(split_top, split)
    write_port(out, join(first, second, split))


def descend(flag, split, w, e):
    a0, a1 = affine(split[0], w, e), affine(split[1], w, e)
    b0, b1 = affine(split[2], w, e), affine(split[3], w, e)
    new_w = (jnp.where(flag, a0, w[0]), jnp.where(flag, a1, w[1]))
    new_e = (jnp.where(flag, e[0], b0), jnp.where(flag, e[1], b1))
    return new_w, new_e


def solve_kernel(own_ref, by1, by3, by2, top_x, pair_x, core, before, low_out, high_out):
    low_bit, high_bit = bits(8)
    first, second = swap_if(low_bit, read_port(own_ref), read_port(by1))
    split_mine = split_of(first, second)
    mine = join(first, second, split_mine)
    first, second = swap_if(low_bit, read_port(by2), read_port(by3))
    theirs = join(first, second, split_of(first, second))
    first, second = swap_if(high_bit, mine, theirs)
    zero = jnp.zeros(TILE, jnp.float32)
    w, e = (zero, zero), (zero, zero)
    w, e = descend(high_bit, split_of(first, second), w, e)
    w, e = descend(low_bit, split_mine, w, e)
    low_bit, high_bit = bits(2)
    w, e = descend(high_bit, read_port(top_x), w, e)
    w, e = descend(low_bit, read_port(pair_x), w, e)
    a0, a1, b0, b1 = (affine(row, w, e) for row in read_port(core))
    for k, value in enumerate((w[0], w[1], b0, b1)):
        low_out[k] = value + value
    for k, value in enumerate((a0, a1, e[0], e[1])):
        high_out[k] = value + value


def combine(ends, spikes, out, stage, sems):
    weights = [ends[k] for k in range(4)]
    copies = []
    size = ROWS // 8 // WRITES
    for piece in range(WRITES):
        for block in range(piece * size, (piece + 1) * size):
            for step in range(8):
                i = 8 * block + step
                value = spikes[0, i]
                for k in range(4):
                    value = value + spikes[k + 1, i] * weights[k]
                stage[block, pl.ds(step, 8, stride=8), :] = value
        span = pl.ds(piece * size, size)
        copy = pltpu.make_async_copy(stage.at[span], out.at[span], sems.at[piece])
        copy.start()
        copies.append(copy)
    for copy in copies:
        copy.wait()


def combine_odd_kernel(ends, spikes, out, stage, sems):
    @pl.when(lax.axis_index("lon") % 2 == 1)
    def _():
        combine(ends, spikes, out, stage, sems)


def combine_even_kernel(ends, spikes, partial, out, stage, sems):
    @pl.when(lax.axis_index("lon") % 2 == 0)
    def _():
        combine(ends, spikes, out, stage, sems)


def call(
    kernel, outs, operands, out_specs=None, in_specs=None, scratch=(), name=None, aliases={}
):
    vmem = pl.BlockSpec(memory_space=pltpu.VMEM)
    return pl.pallas_call(
        kernel,
        out_shape=[jax.ShapeDtypeStruct(shape, jnp.float32) for shape in outs],
        in_specs=in_specs or [vmem] * len(operands),
        out_specs=out_specs or [vmem] * len(outs),
        scratch_shapes=list(scratch),
        compiler_params=pltpu.CompilerParams(vmem_limit_bytes=VMEM_BYTES),
        input_output_aliases=aliases,
        name=name,
    )(*operands)


def exchange(port, odd_mask, even_mask):
    pairs = [(i, i ^ (odd_mask if i % 2 else even_mask)) for i in range(32)]
    return lax.ppermute(port, "lon", pairs)


def per_device(tracer, lower2, lower1, upper1, upper2):
    vmem = pl.BlockSpec(memory_space=pltpu.VMEM)
    hbm = pl.BlockSpec(memory_space=pltpu.HBM)
    tiles = (SUBS, CHUNKS, 64, 128)
    blocks = (SUBS * CHUNKS, 64, 128)

    def view(array):
        return array.reshape(16, 8, 8, 128).transpose(0, 2, 1, 3).reshape(tiles)

    arrays = [
        pltpu.with_memory_space_constraint(view(a), pltpu.HBM)
        for a in (lower2, lower1, upper1, upper2, tracer)
    ]
    port_shape = (20,) + TILE
    port, *loaded = call(
        port_kernel,
        [port_shape] + [tiles] * 5,
        arrays,
        in_specs=[hbm] * 5,
        scratch=[pltpu.SemaphoreType.DMA((5, CHUNKS))],
        name="segment_port",
    )
    chip, core_split = call(
        core_kernel, [port_shape] * 2, [port, exchange(port, 1, 1)], name="core_join"
    )
    x_near, x_end, x_far = (exchange(chip, *masks) for masks in ((3, 3), (6, 8), (4, 8)))
    (spikes,) = call(
        spikes_kernel,
        [(5, ROWS) + TILE],
        loaded + [chip],
        scratch=[pltpu.VMEM((ROWS,) + TILE, jnp.float32)] * 2,
        name="segment_spikes",
    )
    group, pair_x, top_x = call(group_kernel, [port_shape] * 3, [chip, x_near, x_end, x_far], name="x_join")
    y_near, y_end, y_far = (exchange(group, k, 2) for k in (8, 24, 16))
    low_ends, high_ends = call(
        solve_kernel,
        [(4,) + TILE] * 2,
        [group, y_near, y_end, y_far, top_x, pair_x, core_split, spikes],
        name="y_solve",
    )
    received = exchange(low_ends, 1, 1)
    scratch = [pltpu.VMEM(blocks, jnp.float32), pltpu.SemaphoreType.DMA((WRITES,))]
    (out,) = call(
        combine_odd_kernel,
        [blocks],
        [high_ends, spikes],
        out_specs=[hbm],
        scratch=scratch,
        name="combine_odd",
    )
    (out,) = call(
        combine_even_kernel,
        [blocks],
        [received, spikes, out],
        in_specs=[vmem, vmem, hbm],
        out_specs=[hbm],
        scratch=scratch,
        name="combine_even",
        aliases={2: 0},
    )
    return out.reshape(16, 8, 8, 128).transpose(0, 2, 1, 3).reshape(ROWS, 1024)


def solution(mesh):
    spec = P("lon", "lat")
    return jax.shard_map(
        per_device, mesh=mesh, in_specs=(spec,) * 5, out_specs=spec, check_vma=False
    )
```

```python
import jax
import jax.numpy as jnp
from jax import lax
from jax.experimental import pallas as pl
from jax.experimental.pallas import tpu as pltpu
from jax.sharding import PartitionSpec as P

ROWS = 128
SUBS = 2
CHUNKS = 8
WRITES = 8
TILE = (8, 128)
VMEM_BYTES = 12 << 20


def eliminate(state, coefs):
    (far_g, far_a, far_b, far_p, far_q), (near_g, near_a, near_b, near_p, near_q) = state
    low2, low1, up1, up2, target = coefs
    minus_diag = (((low2 + low1) + up1) + up2) - 1.0
    beta = low1 + low2 * far_p
    scale = pl.reciprocal(minus_diag - low2 * far_q - beta * near_p)
    new_g = (low2 * far_g + beta * near_g - target) * scale
    new_a = (low2 * far_a + beta * near_a) * scale
    new_b = (low2 * far_b + beta * near_b) * scale
    new_p = (up1 + beta * near_q) * scale
    new_q = up2 * scale
    return (new_g, new_a, new_b, new_p, new_q)


def eliminate_first(coefs):
    low2, low1, up1, up2, target = coefs
    scale = pl.reciprocal((((low2 + low1) + up1) + up2) - 1.0)
    return (-target * scale, low2 * scale, low1 * scale, up1 * scale, up2 * scale)


def eliminate_second(first, coefs):
    near_g, near_a, near_b, near_p, near_q = first
    low2, low1, up1, up2, target = coefs
    scale = pl.reciprocal((((low2 + low1) + up1) + up2) - 1.0 - low1 * near_p)
    return (
        (low1 * near_g - target) * scale,
        low1 * near_a * scale,
        (low2 + low1 * near_b) * scale,
        (up1 + low1 * near_q) * scale,
        up2 * scale,
    )


def carry_on(head, row):
    g, a, b, p, q = head
    row_g, row_a, row_b, row_p, row_q = row
    return (g + p * row_g, a + p * row_a, b + p * row_b, q + p * row_p, p * row_q)


def affine(row, w, e):
    return row[0] + row[1] * w[0] + row[2] * w[1] + row[3] * e[0] + row[4] * e[1]


def mix(row, left, right):
    return tuple(row[0] * x + row[1] * y for x, y in zip(left, right))


def split_of(first, second):
    r0, r1 = first[2], first[3]
    l0, l1 = second[0], second[1]
    n00 = r0[3] * l0[1] + r0[4] * l1[1]
    n01 = r0[3] * l0[2] + r0[4] * l1[2]
    n10 = r1[3] * l0[1] + r1[4] * l1[1]
    n11 = r1[3] * l0[2] + r1[4] * l1[2]
    d00 = 1.0 - n00
    d11 = 1.0 - n11
    inv = pl.reciprocal(d00 * d11 - n01 * n10)
    k0 = (d11 * inv, n01 * inv)
    k1 = (n10 * inv, d00 * inv)
    s0 = (r0[0] + r0[3] * l0[0] + r0[4] * l1[0], r0[1], r0[2]) + mix(r0[3:5], l0[3:5], l1[3:5])
    s1 = (r1[0] + r1[3] * l0[0] + r1[4] * l1[0], r1[1], r1[2]) + mix(r1[3:5], l0[3:5], l1[3:5])
    a0 = mix(k0, s0, s1)
    a1 = mix(k1, s0, s1)
    b0 = mix(l0[1:3], a0, a1)
    b1 = mix(l1[1:3], a0, a1)
    b0 = (b0[0] + l0[0], b0[1], b0[2], b0[3] + l0[3], b0[4] + l0[4])
    b1 = (b1[0] + l1[0], b1[1], b1[2], b1[3] + l1[3], b1[4] + l1[4])
    return (a0, a1, b0, b1)


def join(first, second, split):
    a0, a1, b0, b1 = split
    left, right = [], []
    for row in first[0:2]:
        far = mix(row[3:5], b0, b1)
        left.append((row[0] + far[0], row[1] + far[1], row[2] + far[2], far[3], far[4]))
    for row in second[2:4]:
        far = mix(row[1:3], a0, a1)
        right.append((row[0] + far[0], far[1], far[2], row[3] + far[3], row[4] + far[4]))
    return tuple(left + right)


def read_port(ref):
    return tuple(tuple(ref[5 * i + j] for j in range(5)) for i in range(4))


def write_port(ref, port):
    for i in range(4):
        for j in range(5):
            ref[5 * i + j] = port[i][j]


def swap_if(flag, one, two):
    first = tuple(tuple(jnp.where(flag, y, x) for x, y in zip(u, v)) for u, v in zip(one, two))
    second = tuple(tuple(jnp.where(flag, x, y) for x, y in zip(u, v)) for u, v in zip(one, two))
    return first, second


def row_of(buffers, sub, chunk, step):
    return tuple(buf[sub, chunk, pl.ds(step, 8, stride=8), :] for buf in buffers)


def place_of(i):
    block, step = divmod(i, 8)
    return block // CHUNKS, block % CHUNKS, step


def port_kernel(*refs):
    sources, out, buffers, sems = refs[0:5], refs[5], refs[6:11], refs[11]
    copies = [
        [
            pltpu.make_async_copy(src.at[:, c], buf.at[:, c], sems.at[i, c])
            for i, (src, buf) in enumerate(zip(sources, buffers))
        ]
        for c in range(CHUNKS)
    ]
    for group in copies:
        for copy in group:
            copy.start()
    far, near = [None] * SUBS, [None] * SUBS
    head0, head1 = [None] * SUBS, [None] * SUBS
    for c in range(CHUNKS):
        for copy in copies[c]:
            copy.wait()
        for step in range(8):
            for s in range(SUBS):
                coefs = row_of(buffers, s, c, step)
                if c == 0 and step == 0:
                    near[s] = eliminate_first(coefs)
                    head0[s] = near[s]
                    continue
                if c == 0 and step == 1:
                    row = eliminate_second(near[s], coefs)
                    head1[s] = row
                else:
                    row = eliminate((far[s], near[s]), coefs)
                    head1[s] = carry_on(head1[s], row)
                head0[s] = carry_on(head0[s], row)
                far[s], near[s] = near[s], row
    ports = []
    for s in range(SUBS):
        g, a, b, p, q = far[s]
        row = near[s]
        tail0 = (g + p * row[0], a + p * row[1], b + p * row[2], q + p * row[3], p * row[4])
        ports.append((head0[s], head1[s], tail0, row))
    while len(ports) > 1:
        ports = [
            join(ports[i], ports[i + 1], split_of(ports[i], ports[i + 1]))
            for i in range(0, len(ports), 2)
        ]
    write_port(out, ports[0])


def spikes_kernel(l2, l1, u1, u2, tr, after, out, p_buf, q_buf):
    buffers = (l2, l1, u1, u2, tr)
    far, near = None, None
    for i in range(ROWS):
        coefs = row_of(buffers, *place_of(i))
        if i == 0:
            row = eliminate_first(coefs)
        elif i == 1:
            row = eliminate_second(near, coefs)
        else:
            row = eliminate((far, near), coefs)
        out[0, i], out[1, i], out[2, i] = row[0], row[1], row[2]
        p_buf[i], q_buf[i] = row[3], row[4]
        far, near = near, row
    zero = jnp.zeros(TILE, jnp.float32)
    one = jnp.ones(TILE, jnp.float32)
    next1 = (zero, zero, zero, one, zero)
    next2 = (zero, zero, zero, zero, one)
    for i in reversed(range(ROWS)):
        p, q = p_buf[i], q_buf[i]
        own = mix((p, q), next1, next2)
        own = (own[0] + out[0, i], own[1] + out[1, i], own[2] + out[2, i], own[3], own[4])
        (target,) = row_of((tr,), *place_of(i))
        out[0, i] = own[0] + own[0] - target
        for k in range(1, 5):
            out[k, i] = own[k]
        next2 = next1
        next1 = own


def core_kernel(own_ref, other_ref, out, split_out):
    is_high = lax.axis_index("lon") % 2 == 1
    first, second = swap_if(is_high, read_port(own_ref), read_port(other_ref))
    split = split_of(first, second)
    write_port(split_out, split)
    write_port(out, join(first, second, split))


def bits(divisor):
    place = (lax.axis_index("lon") // divisor) % 4
    return place % 2 == 1, place // 2 == 1


def group_kernel(own_ref, by1, by3, by2, before, out, split_pair, split_top):
    low_bit, high_bit = bits(2)
    first, second = swap_if(low_bit, read_port(own_ref), read_port(by1))
    split = split_of(first, second)
    write_port(split_pair, split)
    mine = join(first, second, split)
    first, second = swap_if(low_bit, read_port(by2), read_port(by3))
    theirs = join(first, second, split_of(first, second))
    first, second = swap_if(high_bit, mine, theirs)
    split = split_of(first, second)
    write_port(split_top, split)
    write_port(out, join(first, second, split))


def descend(flag, split, w, e):
    a0, a1 = affine(split[0], w, e), affine(split[1], w, e)
    b0, b1 = affine(split[2], w, e), affine(split[3], w, e)
    new_w = (jnp.where(flag, a0, w[0]), jnp.where(flag, a1, w[1]))
    new_e = (jnp.where(flag, e[0], b0), jnp.where(flag, e[1], b1))
    return new_w, new_e


def solve_kernel(own_ref, by1, by3, by2, top_x, pair_x, core, low_out, high_out):
    low_bit, high_bit = bits(8)
    first, second = swap_if(low_bit, read_port(own_ref), read_port(by1))
    split_mine = split_of(first, second)
    mine = join(first, second, split_mine)
    first, second = swap_if(low_bit, read_port(by2), read_port(by3))
    theirs = join(first, second, split_of(first, second))
    first, second = swap_if(high_bit, mine, theirs)
    zero = jnp.zeros(TILE, jnp.float32)
    w, e = (zero, zero), (zero, zero)
    w, e = descend(high_bit, split_of(first, second), w, e)
    w, e = descend(low_bit, split_mine, w, e)
    low_bit, high_bit = bits(2)
    w, e = descend(high_bit, read_port(top_x), w, e)
    w, e = descend(low_bit, read_port(pair_x), w, e)
    a0, a1, b0, b1 = (affine(row, w, e) for row in read_port(core))
    for k, value in enumerate((w[0], w[1], b0, b1)):
        low_out[k] = value + value
    for k, value in enumerate((a0, a1, e[0], e[1])):
        high_out[k] = value + value


def combine(ends, spikes, out, stage, sems):
    weights = [ends[k] for k in range(4)]
    copies = []
    size = ROWS // 8 // WRITES
    for piece in range(WRITES):
        for block in range(piece * size, (piece + 1) * size):
            for step in range(8):
                i = 8 * block + step
                value = spikes[0, i]
                for k in range(4):
                    value = value + spikes[k + 1, i] * weights[k]
                stage[block, pl.ds(step, 8, stride=8), :] = value
        span = pl.ds(piece * size, size)
        copy = pltpu.make_async_copy(stage.at[span], out.at[span], sems.at[piece])
        copy.start()
        copies.append(copy)
    for copy in copies:
        copy.wait()


def combine_odd_kernel(ends, spikes, out, stage, sems):
    @pl.when(lax.axis_index("lon") % 2 == 1)
    def _():
        combine(ends, spikes, out, stage, sems)


def combine_even_kernel(ends, spikes, partial, out, stage, sems):
    @pl.when(lax.axis_index("lon") % 2 == 0)
    def _():
        combine(ends, spikes, out, stage, sems)


def call(
    kernel, outs, operands, out_specs=None, in_specs=None, scratch=(), name=None, aliases={}
):
    vmem = pl.BlockSpec(memory_space=pltpu.VMEM)
    return pl.pallas_call(
        kernel,
        out_shape=[jax.ShapeDtypeStruct(shape, jnp.float32) for shape in outs],
        in_specs=in_specs or [vmem] * len(operands),
        out_specs=out_specs or [vmem] * len(outs),
        scratch_shapes=list(scratch),
        compiler_params=pltpu.CompilerParams(vmem_limit_bytes=VMEM_BYTES),
        input_output_aliases=aliases,
        name=name,
    )(*operands)


def exchange(port, odd_mask, even_mask):
    pairs = [(i, i ^ (odd_mask if i % 2 else even_mask)) for i in range(32)]
    return lax.ppermute(port, "lon", pairs)


def per_device(tracer, lower2, lower1, upper1, upper2):
    vmem = pl.BlockSpec(memory_space=pltpu.VMEM)
    hbm = pl.BlockSpec(memory_space=pltpu.HBM)
    tiles = (SUBS, CHUNKS, 64, 128)
    blocks = (SUBS * CHUNKS, 64, 128)

    def view(array):
        return array.reshape(16, 8, 8, 128).transpose(0, 2, 1, 3).reshape(tiles)

    arrays = [
        pltpu.with_memory_space_constraint(view(a), pltpu.HBM)
        for a in (lower2, lower1, upper1, upper2, tracer)
    ]
    port_shape = (20,) + TILE
    port, *loaded = call(
        port_kernel,
        [port_shape] + [tiles] * 5,
        arrays,
        in_specs=[hbm] * 5,
        scratch=[pltpu.SemaphoreType.DMA((5, CHUNKS))],
        name="segment_port",
    )
    chip, core_split = call(
        core_kernel, [port_shape] * 2, [port, exchange(port, 1, 1)], name="core_join"
    )
    x_near, x_end, x_far = (exchange(chip, k, 8) for k in (2, 6, 4))
    (spikes,) = call(
        spikes_kernel,
        [(5, ROWS) + TILE],
        loaded + [chip],
        scratch=[pltpu.VMEM((ROWS,) + TILE, jnp.float32)] * 2,
        name="segment_spikes",
    )
    group, pair_x, top_x = call(group_kernel, [port_shape] * 3, [chip, x_near, x_end, x_far, spikes], name="x_join")
    y_near, y_end, y_far = (exchange(group, k, 2) for k in (8, 24, 16))
    low_ends, high_ends = call(
        solve_kernel,
        [(4,) + TILE] * 2,
        [group, y_near, y_end, y_far, top_x, pair_x, core_split],
        name="y_solve",
    )
    received = exchange(low_ends, 1, 1)
    scratch = [pltpu.VMEM(blocks, jnp.float32), pltpu.SemaphoreType.DMA((WRITES,))]
    (out,) = call(
        combine_odd_kernel,
        [blocks],
        [high_ends, spikes],
        out_specs=[hbm],
        scratch=scratch,
        name="combine_odd",
    )
    (out,) = call(
        combine_even_kernel,
        [blocks],
        [received, spikes, out],
        in_specs=[vmem, vmem, hbm],
        out_specs=[hbm],
        scratch=scratch,
        name="combine_even",
        aliases={2: 0},
    )
    return out.reshape(16, 8, 8, 128).transpose(0, 2, 1, 3).reshape(ROWS, 1024)


def solution(mesh):
    spec = P("lon", "lat")
    return jax.shard_map(
        per_device, mesh=mesh, in_specs=(spec,) * 5, out_specs=spec, check_vma=False
    )
```
